1024 devices in a mesh: expert: 16 (over z), dp: 8 (over y), tensor: 8 (over x, core).
Axes of the slice: x: 4, y: 8, z: 16, core: 2. Of those that a mesh axis runs over, the one named last changes fastest.
Arguments:
- tokens: bfloat16 [16384, 4096], P(('expert', 'dp')), may hold values from -6 to 6
- out_grad: bfloat16 [16384, 4096], P(('expert', 'dp')), may hold values from -1.1953125 to 1.1953125
- expert_index: int32 [16384, 2], P(('expert', 'dp')), may hold values from 0 to 15, as said below
- slot_index: int32 [16384, 2], P(('expert', 'dp')), may hold values from 0 to 23, as said below
- gate_probs: float32 [16384, 2], P(('expert', 'dp')), may hold values from 0.05 to 0.95
- gate_weight: bfloat16 [16, 4096, 2048], P('expert', None, 'tensor'), may hold values from -0.09375 to 0.09375
- up_weight: bfloat16 [16, 4096, 2048], P('expert', None, 'tensor'), may hold values from -0.09375 to 0.09375
- down_weight: bfloat16 [16, 2048, 4096], P('expert', 'tensor'), may hold values from -0.125 to 0.125
Outputs:
- token_grad: bfloat16 [16384, 4096], P(('expert', 'dp'), 'tensor')
- gate_grad: bfloat16 [16, 4096, 2048], P('expert', 'dp', 'tensor')
- up_grad: bfloat16 [16, 4096, 2048], P('expert', 'dp', 'tensor')
- down_grad: bfloat16 [16, 2048, 4096], P('expert', 'tensor', 'dp')
The draws below stay inside these ranges and needn't reach their ends.
Inputs may be any that keep to these rules, and one draw needn't show every extreme that they name: `expert_index`: in each block of 128 rows (the rows of one device) the two experts of a row differ; in every block one expert is named by exactly 24 rows and no expert by more, and that expert is the same for all blocks of one group. `slot_index`: within one block, the choices that name one expert carry distinct slots that run from 0 to their number minus one; a choice whose slot is 12 or more is dropped.
All inputs are finite; a program needn't handle non-finite values.
Results may differ from the reference program's by a relative error of at most 0.014.
Values may be sent and summed in bfloat16 or wider, within the bound.
No kernel may reach another device: no remote copies, remote signals or barrier semaphores. Data moves between devices by JAX's collectives and lax.ppermute only.
A program may use at most 64 MiB of HBM per device.

```python
import jax
import jax.numpy as jnp
from jax import lax

D = 4096
FF = 2048
TOK_DEV = 128
EXPERTS = 16
CAP = 12
GROUPS = 8
ROWS = 192
TOKENS = 16384
N_EXPERT = 16


def route_block(block_key, hot_expert):
    most_rows = min(2 * CAP, TOK_DEV)
    subkeys = jax.random.split(block_key, 5)
    expert_bias = jax.random.randint(subkeys[0], (EXPERTS, 1), 0, 512)
    cell_noise = jax.random.randint(subkeys[1], (EXPERTS, most_rows), 0, 1024)
    cell_count = EXPERTS * most_rows
    cell_index = jnp.arange(cell_count, dtype=jnp.int32).reshape(EXPERTS, most_rows)
    cell_score = (expert_bias + cell_noise) * cell_count + cell_index
    cell_owner = jnp.arange(EXPERTS, dtype=jnp.int32)[:, None] + 0 * cell_index
    cell_score = jnp.where(cell_owner == hot_expert, cell_score + 4194304, cell_score)
    picked = lax.top_k(cell_score.reshape(-1), 2 * TOK_DEV)[1]
    labels = jnp.sort(cell_owner.reshape(-1)[picked])
    tie_break = jax.random.randint(subkeys[2], (2 * TOK_DEV,), 0, 1024) * (2 * TOK_DEV) + jnp.arange(2 * TOK_DEV, dtype=jnp.int32)
    same_expert = labels[:, None] == labels[None, :]
    slot_value = jnp.sum(same_expert & (tie_break[None, :] < tie_break[:, None]), axis=1).astype(jnp.int32)
    token_order = jax.random.permutation(subkeys[3], TOK_DEV).astype(jnp.int32)
    column_flip = jax.random.randint(subkeys[4], (TOK_DEV,), 0, 2)
    pick_index = jnp.arange(2 * TOK_DEV, dtype=jnp.int32)
    token_of = token_order[pick_index % TOK_DEV]
    column = (pick_index // TOK_DEV + column_flip[token_of]) % 2
    expert_table = jnp.zeros((TOK_DEV, 2), jnp.int32).at[token_of, column].set(labels)
    slot_table = jnp.zeros((TOK_DEV, 2), jnp.int32).at[token_of, column].set(slot_value)
    return (expert_table, slot_table)


def route_all(key):
    base_key = jax.random.fold_in(key, 4242)
    hot_expert = jax.random.randint(jax.random.fold_in(base_key, 1), (GROUPS,), 0, EXPERTS)
    blocks = jnp.arange(TOKENS // TOK_DEV, dtype=jnp.int32)
    block_keys = jax.vmap(lambda block: jax.random.fold_in(base_key, block + 2))(blocks)
    expert_table, slot_table = jax.vmap(route_block)(block_keys, hot_expert[blocks % GROUPS])
    return (expert_table.reshape(TOKENS, 2), slot_table.reshape(TOKENS, 2))


def draw_expert_index(key, part):
    return route_all(key)[0]


def draw_slot_index(key, part):
    return route_all(key)[1]


def shard_levels(key, shape, pieces, low, largest):
    gain, own = 1.0, jax.random.fold_in(key, 6)
    for dim, blocks in pieces:
        steps = jnp.exp(jax.random.uniform(jax.random.fold_in(own, dim), (blocks,), jnp.float32, low / len(pieces), largest / len(pieces)))
        gain = gain * jnp.repeat(steps, shape[dim] // blocks).reshape([-1 if axis == dim else 1 for axis in range(len(shape))])
    return gain


def centred(rng, dims, width, bound, cuts=(), held_as=jnp.bfloat16):
    entries = jax.random.normal(rng, dims, jnp.float32) * width
    if len(cuts) > 0:
        entries = shard_levels(rng, dims, cuts, -0.22, 0.18) * entries
    return jnp.clip(entries, min=-bound, max=bound).astype(held_as)


def setup_inputs(seed: int = 0) -> dict:
    keys = jax.random.split(jax.random.key(seed), 9)
    return {
        "tokens": centred(keys[0], (TOKENS, D), 1.0, 6.0, ((0, 128),)),
        "out_grad": centred(keys[1], (TOKENS, D), 0.2, 1.1953125, ((0, 128),)),
        "expert_index": draw_expert_index(jax.random.fold_in(keys[8], 71), 0),
        "slot_index": draw_slot_index(jax.random.fold_in(keys[8], 71), 0),
        "gate_probs": jnp.clip(0.05 + 0.9 * jax.random.uniform(keys[4], (TOKENS, 2), jnp.float32) ** shard_levels(keys[4], (TOKENS, 2), ((0, 128),), -0.2, 0.2), 0.05, 0.95),
        "gate_weight": centred(keys[5], (EXPERTS, D, FF), D ** -0.5, 0.09375, ((0, 16), (2, 8))),
        "up_weight": centred(keys[6], (EXPERTS, D, FF), D ** -0.5, 0.09375, ((0, 16), (2, 8))),
        "down_weight": centred(keys[7], (EXPERTS, FF, D), FF ** -0.5, 0.125, ((0, 16), (1, 8))),
    }


def reference(tokens, out_grad, expert_index, slot_index, gate_probs, gate_weight, up_weight, down_weight):
    row_index = jnp.arange(TOKENS, dtype=jnp.int32)
    block_index = row_index // TOK_DEV
    group_of = block_index % GROUPS
    source_of = block_index // GROUPS
    total_slots = GROUPS * EXPERTS * ROWS
    kept_mask = slot_index < CAP
    position = ((group_of[:, None] * EXPERTS + expert_index) * N_EXPERT + source_of[:, None]) * CAP + slot_index
    position = jnp.where(kept_mask, position, total_slots).astype(jnp.int32)
    flat_position = position.reshape(-1)
    owners = jnp.repeat(row_index, 2)
    source_row = jnp.full((total_slots + 1,), TOKENS, jnp.int32).at[flat_position].set(owners)[:total_slots]
    source_row = source_row.reshape(GROUPS, EXPERTS, ROWS)
    slot_prob = jnp.zeros((total_slots + 1,), jnp.float32).at[flat_position].set(gate_probs.reshape(-1).astype(jnp.float32))[:total_slots]
    slot_prob = slot_prob.reshape(GROUPS, EXPERTS, ROWS)
    padded_tokens = jnp.concatenate([tokens, jnp.zeros((1, D), tokens.dtype)], axis=0)
    padded_grads = jnp.concatenate([out_grad, jnp.zeros((1, D), out_grad.dtype)], axis=0)
    contract_last = (((1,), (1,)), ((), ()))
    contract_first = (((0,), (0,)), ((), ()))

    def expert_pass(expert):
        gate_matrix = gate_weight[expert]
        up_matrix = up_weight[expert]
        down_matrix = down_weight[expert]

        def group_pass(group_index):
            picked = source_row[group_index, expert]
            routed = padded_tokens[picked]
            scaled = (slot_prob[group_index, expert][:, None] * padded_grads[picked].astype(jnp.float32)).astype(jnp.bfloat16)
            gate_value = jnp.dot(routed, gate_matrix, preferred_element_type=jnp.float32)
            up_value = jnp.dot(routed, up_matrix, preferred_element_type=jnp.float32)
            gate_sigmoid = jax.nn.sigmoid(gate_value)
            activated = gate_value * gate_sigmoid
            hidden = (activated * up_value).astype(jnp.bfloat16)
            back_grad = lax.dot_general(scaled, down_matrix, contract_last, preferred_element_type=jnp.float32)
            gate_delta = (back_grad * up_value * gate_sigmoid * (1.0 + gate_value * (1.0 - gate_sigmoid))).astype(jnp.bfloat16)
            up_delta = (back_grad * activated).astype(jnp.bfloat16)
            slot_grad = lax.dot_general(gate_delta, gate_matrix, contract_last, preferred_element_type=jnp.float32)
            slot_grad = slot_grad + lax.dot_general(up_delta, up_matrix, contract_last, preferred_element_type=jnp.float32)
            part_gate = lax.dot_general(routed, gate_delta, contract_first, preferred_element_type=jnp.float32).astype(jnp.bfloat16)
            part_up = lax.dot_general(routed, up_delta, contract_first, preferred_element_type=jnp.float32).astype(jnp.bfloat16)
            part_down = lax.dot_general(hidden, scaled, contract_first, preferred_element_type=jnp.float32).astype(jnp.bfloat16)
            return slot_grad, part_gate, part_up, part_down

        slot_grad, part_gate, part_up, part_down = lax.map(group_pass, jnp.arange(GROUPS, dtype=jnp.int32))
        gate_total = jnp.sum(part_gate.astype(jnp.float32), axis=0).astype(jnp.bfloat16)
        up_total = jnp.sum(part_up.astype(jnp.float32), axis=0).astype(jnp.bfloat16)
        down_total = jnp.sum(part_down.astype(jnp.float32), axis=0).astype(jnp.bfloat16)
        return slot_grad, gate_total, up_total, down_total

    slot_grad, gate_grad, up_grad, down_grad = lax.map(expert_pass, jnp.arange(EXPERTS, dtype=jnp.int32))
    flat_grad = jnp.transpose(slot_grad, (1, 0, 2, 3)).reshape(total_slots, D)
    safe_position = jnp.minimum(position, total_slots - 1).astype(jnp.int32)
    chosen = jnp.where(kept_mask[:, :, None], flat_grad[safe_position], jnp.zeros((), flat_grad.dtype))
    token_grad = jnp.sum(chosen, axis=1).astype(jnp.bfloat16)
    return (token_grad, gate_grad, up_grad, down_grad)
```

```python
import jax
import jax.numpy as jnp
from jax import lax
from jax.experimental import pallas as pl
from jax.experimental.pallas import tpu as pltpu
from jax.sharding import PartitionSpec as P

BF = jnp.bfloat16
F32 = jnp.float32
VM = pl.BlockSpec(memory_space=pltpu.VMEM)
HB = pl.BlockSpec(memory_space=pltpu.HBM)
SM = pl.BlockSpec(memory_space=pltpu.SMEM)
LAST = (((1,), (1,)), ((), ()))
FIRST = (((0,), (0,)), ((), ()))
TENSOR = 8
RIGHT = [(t, (t + 2) % TENSOR) for t in range(TENSOR)]
LEFT = [(t, (t - 2) % TENSOR) for t in range(TENSOR)]
SWAP = [(t, t ^ 1) for t in range(TENSOR)]


def row_targets(ei, si, q):
    base = ei * 24
    near = base + q * 8 + si
    far = base + 16 + q * 4 + (si - 8)
    return jnp.where(si < 12, jnp.where(si < 8, near, far), -1)


def picks(ei_ref, si_ref, q):
    rows = lax.broadcasted_iota(jnp.int32, (384, 128), 0)
    target = row_targets(ei_ref[...], si_ref[...], q)
    return [rows == target[k : k + 1, :] for k in range(2)]


def far_rows(q):
    row = lax.broadcasted_iota(jnp.int32, (64, 128), 0)
    col = lax.broadcasted_iota(jnp.int32, (64, 128), 1)
    return (col == (row >> 2) * 8 + q * 4 + (row & 3)).astype(BF)


def dispatch_kernel(t_ref, ei_ref, si_ref, prob_ref, tok_hbm, grad_hbm, out_ref, buf, sem):
    t = t_ref[0]
    unit = lax.rem(t, 4)

    def fetch(src):
        for k in range(8):
            q, j = k // 4, k % 4
            pltpu.make_async_copy(
                src.at[:, pl.ds(pl.multiple_of(k * 512 + unit * 128, 128), 128)],
                buf.at[pl.ds(q * 128, 128), pl.ds(j * 128, 128)],
                sem.at[k],
            ).start()
        for k in range(8):
            q, j = k // 4, k % 4
            pltpu.make_async_copy(
                src.at[:, pl.ds(pl.multiple_of(k * 512 + unit * 128, 128), 128)],
                buf.at[pl.ds(q * 128, 128), pl.ds(j * 128, 128)],
                sem.at[k],
            ).wait()

    @pl.when(t < 4)
    def _():
        fetch(tok_hbm)

    @pl.when(t >= 4)
    def _():
        fetch(grad_hbm)

    masks, weight = [], jnp.zeros((384, 1), F32)
    for q in range(2):
        first, second = picks(ei_ref, si_ref, q)
        prob = jnp.where(first, prob_ref[0:1, :], 0.0) + jnp.where(second, prob_ref[1:2, :], 0.0)
        weight = weight + jnp.sum(prob, axis=1, keepdims=True)
        masks.append(jnp.logical_or(first, second).astype(F32).astype(BF))
    rows = jnp.dot(jnp.concatenate(masks, axis=1), buf[...], preferred_element_type=F32)
    weight = jnp.where(t < 4, jnp.ones_like(weight), weight)
    out_ref[...] = (rows * weight).astype(BF)


def unpack(block, q, far):
    near = block[:, q * 8 : (q + 1) * 8, :].reshape(128, block.shape[2])
    rest = block[:, 16:24, :].reshape(128, block.shape[2])
    rest = jnp.dot(far, rest, preferred_element_type=F32).astype(BF)
    return jnp.concatenate([near, rest], axis=0)


def forward_kernel(g_hbm, wg_hbm, wu_hbm, wd_hbm, out_ref, buf, wg, wu, wd, sem):
    copies = [
        [
            pltpu.make_async_copy(g_hbm.at[t], buf.at[t], sem.at[0, t]),
            *(
                pltpu.make_async_copy(src.at[:, t % 4], dst.at[:, t % 4], sem.at[side + 1, t])
                for side, (src, dst) in enumerate(((wg_hbm, wg), (wu_hbm, wu)))
                if t < 4
            ),
        ]
        for t in range(8)
    ]
    copies[4].append(pltpu.make_async_copy(wd_hbm, wd, sem.at[1, 4]))
    for group in copies:
        for copy in group:
            copy.start()
    far = [far_rows(q) for q in range(2)]
    gate = up = back = jnp.zeros((192, 256), F32)
    for t in range(8):
        for copy in copies[t]:
            copy.wait()
        unit = t % 4
        x = jnp.concatenate([unpack(buf[t], q, far[q]) for q in range(2)], axis=1)
        if t < 4:
            gate += jnp.dot(x, wg[:, unit].reshape(1024, 256), preferred_element_type=F32)
            up += jnp.dot(x, wu[:, unit].reshape(1024, 256), preferred_element_type=F32)
        else:
            w = jnp.concatenate(
                [wd[:, pl.ds(k * 512 + unit * 128, 128)] for k in range(8)], axis=1
            )
            back += lax.dot_general(x, w, LAST, preferred_element_type=F32)
    sig = jax.nn.sigmoid(gate)
    act = gate * sig
    out_ref[:, 0:256] = (back * up * sig * (1.0 + gate * (1.0 - sig))).astype(BF)
    out_ref[:, 256:512] = (back * act).astype(BF)
    out_ref[:, 512:768] = (act * up).astype(BF)


def slot_kernel(delta_ref, wg_hbm, wu_hbm, out_ref, wg, wu, sem):
    copies = [
        [
            pltpu.make_async_copy(src.at[k], dst.at[k], sem.at[side, k])
            for side, (src, dst) in enumerate(((wg_hbm, wg), (wu_hbm, wu)))
        ]
        for k in range(8)
    ]
    for group in copies:
        for copy in group:
            copy.start()
    for k in range(8):
        for copy in copies[k]:
            copy.wait()
        term = lax.dot_general(
            delta_ref[:, 0:256], wg[k].reshape(512, 256), LAST, preferred_element_type=F32
        ) + lax.dot_general(
            delta_ref[:, 256:512], wu[k].reshape(512, 256), LAST, preferred_element_type=F32
        )
        out_ref[k] = term.astype(BF)


def pack_kernel(parts_ref, out_ref):
    total = parts_ref[0].astype(F32)
    for t in range(1, 8):
        total = total + parts_ref[t].astype(F32)
    rows = total.astype(BF)
    rest = jnp.zeros((128, 256), F32)
    for q in range(2):
        half = rows[:, q * 256 : (q + 1) * 256]
        out_ref[:, q * 8 : (q + 1) * 8, :] = half[0:128].reshape(16, 8, 256)
        rest += lax.dot_general(far_rows(q), half[128:192], FIRST, preferred_element_type=F32)
    out_ref[:, 16:24, :] = rest.astype(BF).reshape(16, 8, 256)


def combine_kernel(ei_ref, si_ref, ret_ref, out_ref):
    for q in range(2):
        first, second = picks(ei_ref, si_ref, q)
        mask = jnp.logical_or(first, second).astype(F32).astype(BF)
        out_ref[:, q * 256 : (q + 1) * 256] = lax.dot_general(
            mask, ret_ref[...], FIRST, preferred_element_type=F32
        ).astype(BF)


def corner_kernel(block_ref, out_ref):
    for q in range(2):
        x = unpack(block_ref[...], q, far_rows(q))
        for j in range(4):
            out_ref[q * 4 + j] = x[:, j * 128 : (j + 1) * 128]


def weight_kernel(t_ref, delta_ref, own_hbm, other_hbm, gate_ref, up_ref, down_ref, buf, sem):
    t = t_ref[0]
    core = lax.rem(t, 2)
    chip = lax.div(t, 2)
    copies = []
    for side, src in enumerate((own_hbm, other_hbm)):
        for place, shift in enumerate((0, 3, 1, 2)):
            at = lax.rem(chip + shift, 4) * 2 + (core if side == 0 else 1 - core)
            copies.append(
                pltpu.make_async_copy(src.at[place], buf.at[at], sem.at[side * 4 + place])
            )
    for copy in copies:
        copy.start()
    for copy in copies:
        copy.wait()
    tok = jnp.concatenate([buf[u].reshape(1536, 128) for u in range(4)], axis=1)
    both = lax.dot_general(tok, delta_ref[:, 0:512], FIRST, preferred_element_type=F32)
    gate_ref[...] = both[:, 0:256].astype(BF)
    up_ref[...] = both[:, 256:512].astype(BF)
    grad = jnp.concatenate([buf[4 + u].reshape(1536, 128) for u in range(4)], axis=1)
    down_ref[...] = lax.dot_general(
        delta_ref[:, 512:768], grad, FIRST, preferred_element_type=F32
    ).astype(BF)


def call(kernel, out, specs, scratch=(), flops=0, size=0):
    single = not isinstance(out, (list, tuple))
    return pl.pallas_call(
        kernel,
        out_shape=out,
        in_specs=specs,
        out_specs=VM if single else [VM] * len(out),
        scratch_shapes=scratch,
        cost_estimate=pl.CostEstimate(flops=flops, bytes_accessed=size, transcendentals=0),
        compiler_params=pltpu.CompilerParams(vmem_limit_bytes=67_043_328),
    )


def shape(dims, kind=BF):
    return jax.ShapeDtypeStruct(dims, kind)


def on_device(tokens, out_grad, expert_index, slot_index, gate_probs, gate_weight, up_weight, down_weight):
    t = lax.axis_index("tensor").astype(jnp.int32).reshape(1)
    ei, si, prob = expert_index.T, slot_index.T, gate_probs.T
    wg = gate_weight.reshape(8, 4, 128, 256)
    wu = up_weight.reshape(8, 4, 128, 256)
    wd = down_weight[0]
    dma = pltpu.SemaphoreType.DMA

    sent = call(
        dispatch_kernel,
        shape((384, 512)),
        [SM, VM, VM, VM, HB, HB],
        [pltpu.VMEM((256, 512), BF), dma((8,))],
        flops=100_000_000,
        size=700_000,
    )(t, ei, si, prob, tokens, out_grad)
    block = lax.all_to_all(sent.reshape(16, 24, 512), "expert", 0, 0, tiled=True)
    whole = lax.all_gather(block.reshape(384, 512), "tensor", axis=0, tiled=True)

    corner = call(
        corner_kernel, shape((8, 192, 128)), [VM], flops=20_000_000, size=800_000
    )(block)
    mine = lax.all_to_all(corner, "dp", 0, 0, tiled=True)
    from_left = lax.ppermute(mine, "tensor", RIGHT)
    from_right = lax.ppermute(mine, "tensor", LEFT)

    whole, from_left, from_right = lax.optimization_barrier((whole, from_left, from_right))
    delta = call(
        forward_kernel,
        shape((192, 768)),
        [HB, HB, HB, HB],
        [
            pltpu.VMEM((8, 16, 24, 512), BF),
            pltpu.VMEM((8, 4, 128, 256), BF),
            pltpu.VMEM((8, 4, 128, 256), BF),
            pltpu.VMEM((256, 4096), BF),
            dma((3, 8)),
        ],
        flops=1_300_000_000,
        size=10_000_000,
    )(whole.reshape(8, 16, 24, 512), wg, wu, wd)
    far_low = lax.ppermute(from_left[0:4], "tensor", RIGHT)
    far_high = lax.ppermute(from_right[4:8], "tensor", LEFT)
    own = jnp.concatenate([mine, from_left, from_right, far_low, far_high], axis=0)
    other = lax.ppermute(own, "tensor", SWAP)
    deltas = lax.all_gather(delta, "dp", axis=0, tiled=True)

    terms = call(
        slot_kernel,
        shape((8, 192, 512)),
        [VM, HB, HB],
        [pltpu.VMEM((8, 4, 128, 256), BF), pltpu.VMEM((8, 4, 128, 256), BF), dma((2, 8))],
        flops=800_000_000,
        size=6_000_000,
    )(delta, wg, wu)
    parts = lax.all_to_all(terms, "tensor", 0, 0, tiled=True)
    back = call(pack_kernel, shape((16, 24, 256)), [VM], flops=10_000_000, size=1_800_000)(parts)
    returned = lax.all_to_all(back, "expert", 0, 0, tiled=True)
    token_grad = call(
        combine_kernel, shape((128, 512)), [VM, VM, VM], flops=50_000_000, size=400_000
    )(ei, si, returned.reshape(384, 256))

    gate_grad, up_grad, down_grad = call(
        weight_kernel,
        [shape((512, 256)), shape((512, 256)), shape((256, 512))],
        [SM, VM, HB, HB],
        [pltpu.VMEM((8, 8, 192, 128), BF), dma((8,))],
        flops=1_200_000_000,
        size=6_000_000,
    )(t, deltas, own.reshape(4, 8, 192, 128), other.reshape(4, 8, 192, 128))
    return (token_grad, gate_grad[None], up_grad[None], down_grad[None])


def solution(mesh):
    rows = P(("expert", "dp"), None)
    return jax.shard_map(
        on_device,
        mesh=mesh,
        in_specs=(
            rows,
            rows,
            rows,
            rows,
            rows,
            P("expert", None, "tensor"),
            P("expert", None, "tensor"),
            P("expert", "tensor", None),
        ),
        out_specs=(
            P(("expert", "dp"), "tensor"),
            P("expert", "dp", "tensor"),
            P("expert", "dp", "tensor"),
            P("expert", "tensor", "dp"),
        ),
        check_vma=False,
    )
```

```python
import jax
import jax.numpy as jnp
from jax import lax
from jax.experimental import pallas as pl
from jax.experimental.pallas import tpu as pltpu
from jax.sharding import PartitionSpec as P


BF = jnp.bfloat16
F32 = jnp.float32
VM = pl.BlockSpec(memory_space=pltpu.VMEM)
HB = pl.BlockSpec(memory_space=pltpu.HBM)
SM = pl.BlockSpec(memory_space=pltpu.SMEM)
LAST = (((1,), (1,)), ((), ()))
FIRST = (((0,), (0,)), ((), ()))
TENSOR = 8
SIDE = [(t, (t + (2 if t % 2 == 0 else -2)) % TENSOR) for t in range(TENSOR)]
FAR = [(t, (t + 4) % TENSOR) for t in range(TENSOR)]
SWAP = [(t, t ^ 1) for t in range(TENSOR)]


def row_targets(ei, si, q):
    base = ei * 24
    near = base + q * 8 + si
    far = base + 16 + q * 4 + (si - 8)
    return jnp.where(si < 12, jnp.where(si < 8, near, far), -1)


def picks(ei_ref, si_ref, q):
    rows = lax.broadcasted_iota(jnp.int32, (384, 128), 0)
    target = row_targets(ei_ref[...], si_ref[...], q)
    return [rows == target[k : k + 1, :] for k in range(2)]


def far_rows(q):
    row = lax.broadcasted_iota(jnp.int32, (64, 128), 0)
    col = lax.broadcasted_iota(jnp.int32, (64, 128), 1)
    return (col == (row >> 2) * 8 + q * 4 + (row & 3)).astype(BF)


def dispatch_kernel(t_ref, ei_ref, si_ref, prob_ref, tok_hbm, grad_hbm, out_ref, buf, sem):
    t = t_ref[0]
    unit = lax.rem(t, 4)

    def fetch(src):
        for k in range(8):
            q, j = k // 4, k % 4
            pltpu.make_async_copy(
                src.at[:, pl.ds(pl.multiple_of(k * 512 + unit * 128, 128), 128)],
                buf.at[pl.ds(q * 128, 128), pl.ds(j * 128, 128)],
                sem.at[k],
            ).start()
        for k in range(8):
            q, j = k // 4, k % 4
            pltpu.make_async_copy(
                src.at[:, pl.ds(pl.multiple_of(k * 512 + unit * 128, 128), 128)],
                buf.at[pl.ds(q * 128, 128), pl.ds(j * 128, 128)],
                sem.at[k],
            ).wait()

    @pl.when(t < 4)
    def _():
        fetch(tok_hbm)

    @pl.when(t >= 4)
    def _():
        fetch(grad_hbm)

    masks, weight = [], jnp.zeros((384, 1), F32)
    for q in range(2):
        first, second = picks(ei_ref, si_ref, q)
        prob = jnp.where(first, prob_ref[0:1, :], 0.0) + jnp.where(second, prob_ref[1:2, :], 0.0)
        weight = weight + jnp.sum(prob, axis=1, keepdims=True)
        masks.append(jnp.logical_or(first, second).astype(F32).astype(BF))
    rows = jnp.dot(jnp.concatenate(masks, axis=1), buf[...], preferred_element_type=F32)
    weight = jnp.where(t < 4, jnp.ones_like(weight), weight)
    out_ref[...] = (rows * weight).astype(BF)


def unpack(block, q, far):
    near = block[:, q * 8 : (q + 1) * 8, :].reshape(128, block.shape[2])
    rest = block[:, 16:24, :].reshape(128, block.shape[2])
    rest = jnp.dot(far, rest, preferred_element_type=F32).astype(BF)
    return jnp.concatenate([near, rest], axis=0)


def settle(low, high):
    near = low[0:128] + high[0:128]
    width = low.shape[1]
    far = low[128:256].reshape(16, 8, width)
    far = far + pltpu.roll(high[128:256].reshape(16, 8, width), 4, 1)
    pairs = far.reshape(8, 2, 8, width)
    row = lax.broadcasted_iota(jnp.int32, (8, 8, width), 1)
    rest = jnp.where(row < 4, pairs[:, 0], pltpu.roll(pairs[:, 1], 4, 1)).reshape(64, width)
    return jnp.concatenate([near, rest], axis=0)


def forward_kernel(g_hbm, wg_hbm, wu_hbm, wd_hbm, out_ref, buf, wg, wu, wd, sem):
    copies = [pltpu.make_async_copy(g_hbm.at[t], buf.at[t], sem.at[0, t]) for t in range(8)]
    down = [
        pltpu.make_async_copy(
            wd_hbm.at[:, pl.ds(q * 2048, 2048)], wd.at[:, pl.ds(q * 2048, 2048)], sem.at[1, q]
        )
        for q in range(2)
    ]
    first = [
        [
            pltpu.make_async_copy(
                src.at[pl.ds(q * 4, 4)], dst.at[pl.ds(q * 4, 4)], sem.at[2 + side, q]
            )
            for side, (src, dst) in enumerate(((wg_hbm, wg), (wu_hbm, wu)))
        ]
        for q in range(2)
    ]
    for copy in copies[4:8] + down + copies[0:4] + first[0] + first[1]:
        copy.start()

    def rows(units, q):
        return jnp.concatenate(
            [
                jnp.concatenate(
                    [
                        buf[t, :, q * 8 : (q + 1) * 8, :].reshape(128, 512),
                        buf[t, :, 16:24, :].reshape(128, 512),
                    ],
                    axis=0,
                )
                for t in units
            ],
            axis=1,
        )

    for copy in copies[4:8]:
        copy.wait()
    terms = []
    for q in range(2):
        down[q].wait()
        w = jnp.concatenate(
            [
                wd[:, (q * 4 + j) * 512 + unit * 128 : (q * 4 + j) * 512 + (unit + 1) * 128]
                for unit in range(4)
                for j in range(4)
            ],
            axis=1,
        )
        terms.append(
            lax.dot_general(rows(range(4, 8), q), w, LAST, preferred_element_type=F32)
        )
    back = settle(*terms)
    for copy in copies[0:4]:
        copy.wait()
    terms = []
    for q in range(2):
        for copy in first[q]:
            copy.wait()
        w = jnp.concatenate(
            [
                jnp.concatenate(
                    [m[q * 4 : (q + 1) * 4, unit].reshape(512, 256) for unit in range(4)], axis=0
                )
                for m in (wg, wu)
            ],
            axis=1,
        )
        terms.append(jnp.dot(rows(range(4), q), w, preferred_element_type=F32))
    both = settle(*terms)
    gate, up = both[:, 0:256], both[:, 256:512]
    sig = jax.nn.sigmoid(gate)
    act = gate * sig
    out_ref[:, 0:256] = (back * up * sig * (1.0 + gate * (1.0 - sig))).astype(BF)
    out_ref[:, 256:512] = (back * act).astype(BF)
    out_ref[:, 512:768] = (act * up).astype(BF)


def slot_kernel(delta_ref, wg_hbm, wu_hbm, out_ref, wg, wu, sem):
    copies = [
        [
            pltpu.make_async_copy(src.at[k], dst.at[k], sem.at[side, k])
            for side, (src, dst) in enumerate(((wg_hbm, wg), (wu_hbm, wu)))
        ]
        for k in range(8)
    ]
    for group in copies:
        for copy in group:
            copy.start()
    for k in range(8):
        for copy in copies[k]:
            copy.wait()
        w = jnp.concatenate([wg[k].reshape(512, 256), wu[k].reshape(512, 256)], axis=1)
        term = lax.dot_general(delta_ref[:, 0:512], w, LAST, preferred_element_type=F32)
        out_ref[k] = term.astype(BF)


def pack_kernel(parts_ref, out_ref):
    total = parts_ref[0].astype(F32)
    for t in range(1, 8):
        total = total + parts_ref[t].astype(F32)
    rows = total.astype(BF)
    rest = jnp.zeros((128, 256), F32)
    for q in range(2):
        half = rows[:, q * 256 : (q + 1) * 256]
        out_ref[:, q * 8 : (q + 1) * 8, :] = half[0:128].reshape(16, 8, 256)
        rest += lax.dot_general(far_rows(q), half[128:192], FIRST, preferred_element_type=F32)
    out_ref[:, 16:24, :] = rest.astype(BF).reshape(16, 8, 256)


def combine_kernel(ei_ref, si_ref, ret_ref, out_ref):
    for q in range(2):
        first, second = picks(ei_ref, si_ref, q)
        mask = jnp.logical_or(first, second).astype(F32).astype(BF)
        out_ref[:, q * 256 : (q + 1) * 256] = lax.dot_general(
            mask, ret_ref[...], FIRST, preferred_element_type=F32
        ).astype(BF)


def corner_kernel(block_ref, out_ref):
    for q in range(2):
        x = unpack(block_ref[...], q, far_rows(q))
        for j in range(4):
            out_ref[q * 4 + j] = x[:, j * 128 : (j + 1) * 128]


def weight_kernel(t_ref, delta_ref, pair_hbm, side_hbm, side2_hbm, far_hbm, far2_hbm, gate_ref, up_ref, down_ref, buf, sem):
    t = t_ref[0]
    core = lax.rem(t, 2)
    chip = lax.div(t, 2)
    near = jnp.where(core == 0, 3, 1)
    places = [
        (pair_hbm.at[0], 0, core),
        (pair_hbm.at[1], 0, 1 - core),
        (side_hbm.at[0], near, core),
        (side_hbm.at[1], near, 1 - core),
        (side2_hbm.at[0], 4 - near, 1 - core),
        (side2_hbm.at[1], 4 - near, core),
        (far_hbm, 2, core),
        (far2_hbm, 2, 1 - core),
    ]
    copies = [
        pltpu.make_async_copy(src, buf.at[lax.rem(chip + shift, 4) * 2 + which], sem.at[i])
        for i, (src, shift, which) in enumerate(places)
    ]
    for copy in copies:
        copy.start()
    for copy in copies:
        copy.wait()
    tok = jnp.concatenate([buf[u].reshape(1536, 128) for u in range(4)], axis=1)
    both = lax.dot_general(tok, delta_ref[:, 0:512], FIRST, preferred_element_type=F32)
    gate_ref[...] = both[:, 0:256].astype(BF)
    up_ref[...] = both[:, 256:512].astype(BF)
    grad = jnp.concatenate([buf[4 + u].reshape(1536, 128) for u in range(4)], axis=1)
    down_ref[...] = lax.dot_general(
        delta_ref[:, 512:768], grad, FIRST, preferred_element_type=F32
    ).astype(BF)


def call(kernel, out, specs, scratch=(), flops=0, size=0):
    single = not isinstance(out, (list, tuple))
    return pl.pallas_call(
        kernel,
        out_shape=out,
        in_specs=specs,
        out_specs=VM if single else [VM] * len(out),
        scratch_shapes=scratch,
        cost_estimate=pl.CostEstimate(flops=flops, bytes_accessed=size, transcendentals=0),
        compiler_params=pltpu.CompilerParams(vmem_limit_bytes=67_043_328),
    )


def shape(dims, kind=BF):
    return jax.ShapeDtypeStruct(dims, kind)


def layer(tokens, out_grad, expert_index, slot_index, gate_probs, gate_weight, up_weight, down_weight):
    t = lax.axis_index("tensor").astype(jnp.int32).reshape(1)
    ei, si, prob = expert_index.T, slot_index.T, gate_probs.T
    wg = gate_weight.reshape(8, 4, 128, 256)
    wu = up_weight.reshape(8, 4, 128, 256)
    wd = down_weight[0]
    dma = pltpu.SemaphoreType.DMA

    sent = call(
        dispatch_kernel,
        shape((384, 512)),
        [SM, VM, VM, VM, HB, HB],
        [pltpu.VMEM((256, 512), BF), dma((8,))],
        flops=100_000_000,
        size=700_000,
    )(t, ei, si, prob, tokens, out_grad)
    block = lax.all_to_all(sent.reshape(16, 24, 512), "expert", 0, 0, tiled=True)
    whole = lax.all_gather(block.reshape(384, 512), "tensor", axis=0, tiled=True)

    corner = call(
        corner_kernel, shape((8, 192, 128)), [VM], flops=20_000_000, size=800_000
    )(block)
    mine = lax.all_to_all(corner, "dp", 0, 0, tiled=True)
    turned = lax.ppermute(mine, "tensor", SWAP)
    pair = jnp.concatenate([mine[None], turned[None]], axis=0)
    side = lax.ppermute(pair, "tensor", SIDE)
    far = lax.ppermute(mine, "tensor", FAR)
    whole, pair = lax.optimization_barrier((whole, pair))
    delta = call(
        forward_kernel,
        shape((192, 768)),
        [HB, HB, HB, HB],
        [
            pltpu.VMEM((8, 16, 24, 512), BF),
            pltpu.VMEM((8, 4, 128, 256), BF),
            pltpu.VMEM((8, 4, 128, 256), BF),
            pltpu.VMEM((256, 4096), BF),
            dma((4, 8)),
        ],
        flops=1_300_000_000,
        size=10_000_000,
    )(whole.reshape(8, 16, 24, 512), wg, wu, wd)
    side2 = lax.ppermute(side, "tensor", SWAP)
    far2 = lax.ppermute(far, "tensor", SWAP)
    deltas = lax.all_gather(delta, "dp", axis=0, tiled=True)

    terms = call(
        slot_kernel,
        shape((8, 192, 512)),
        [VM, HB, HB],
        [pltpu.VMEM((8, 4, 128, 256), BF), pltpu.VMEM((8, 4, 128, 256), BF), dma((2, 8))],
        flops=800_000_000,
        size=6_000_000,
    )(delta, wg, wu)
    parts = lax.all_to_all(terms, "tensor", 0, 0, tiled=True)
    back = call(pack_kernel, shape((16, 24, 256)), [VM], flops=10_000_000, size=1_800_000)(parts)
    returned = lax.all_to_all(back, "expert", 0, 0, tiled=True)
    gate_grad, up_grad, down_grad = call(
        weight_kernel,
        [shape((512, 256)), shape((512, 256)), shape((256, 512))],
        [SM, VM, HB, HB, HB, HB, HB],
        [pltpu.VMEM((8, 8, 192, 128), BF), dma((8,))],
        flops=1_200_000_000,
        size=6_000_000,
    )(t, deltas, pair, side, side2, far, far2)
    returned, gate_grad = lax.optimization_barrier((returned, gate_grad))
    token_grad = call(
        combine_kernel, shape((128, 512)), [VM, VM, VM], flops=50_000_000, size=400_000
    )(ei, si, returned.reshape(384, 256))
    return (token_grad, gate_grad[None], up_grad[None], down_grad[None])


def solution(mesh):
    rows = P(("expert", "dp"), None)
    return jax.shard_map(
        layer,
        mesh=mesh,
        in_specs=(
            rows,
            rows,
            rows,
            rows,
            rows,
            P("expert", None, "tensor"),
            P("expert", None, "tensor"),
            P("expert", "tensor", None),
        ),
        out_specs=(
            P(("expert", "dp"), "tensor"),
            P("expert", "dp", "tensor"),
            P("expert", "dp", "tensor"),
            P("expert", "tensor", "dp"),
        ),
        check_vma=False,
    )
```

```python
import jax
import jax.numpy as jnp
from jax import lax
from jax.experimental import pallas as pl
from jax.experimental.pallas import tpu as pltpu
from jax.sharding import PartitionSpec as P


BF = jnp.bfloat16
F32 = jnp.float32
VM = pl.BlockSpec(memory_space=pltpu.VMEM)
HB = pl.BlockSpec(memory_space=pltpu.HBM)
SM = pl.BlockSpec(memory_space=pltpu.SMEM)
LAST = (((1,), (1,)), ((), ()))
FIRST = (((0,), (0,)), ((), ()))
TENSOR = 8
SIDE = [(t, (t + (2 if t % 2 == 0 else -2)) % TENSOR) for t in range(TENSOR)]
FAR = [(t, (t + 4) % TENSOR) for t in range(TENSOR)]
SWAP = [(t, t ^ 1) for t in range(TENSOR)]


def row_targets(ei, si, q):
    base = ei * 24
    near = base + q * 8 + si
    far = base + 16 + q * 4 + (si - 8)
    return jnp.where(si < 12, jnp.where(si < 8, near, far), -1)


def picks(ei_ref, si_ref, q):
    rows = lax.broadcasted_iota(jnp.int32, (384, 128), 0)
    target = row_targets(ei_ref[...], si_ref[...], q)
    return [rows == target[k : k + 1, :] for k in range(2)]


def far_rows(q):
    row = lax.broadcasted_iota(jnp.int32, (64, 128), 0)
    col = lax.broadcasted_iota(jnp.int32, (64, 128), 1)
    return (col == (row >> 2) * 8 + q * 4 + (row & 3)).astype(BF)


def dispatch_kernel(t_ref, ei_ref, si_ref, prob_ref, tok_hbm, grad_hbm, out_ref, buf, sem):
    t = t_ref[0]
    unit = lax.rem(t, 4)

    def fetch(src):
        for k in range(8):
            q, j = k // 4, k % 4
            pltpu.make_async_copy(
                src.at[:, pl.ds(pl.multiple_of(k * 512 + unit * 128, 128), 128)],
                buf.at[pl.ds(q * 128, 128), pl.ds(j * 128, 128)],
                sem.at[k],
            ).start()
        for k in range(8):
            q, j = k // 4, k % 4
            pltpu.make_async_copy(
                src.at[:, pl.ds(pl.multiple_of(k * 512 + unit * 128, 128), 128)],
                buf.at[pl.ds(q * 128, 128), pl.ds(j * 128, 128)],
                sem.at[k],
            ).wait()

    @pl.when(t < 4)
    def _():
        fetch(tok_hbm)

    @pl.when(t >= 4)
    def _():
        fetch(grad_hbm)

    masks, weight = [], jnp.zeros((384, 1), F32)
    for q in range(2):
        first, second = picks(ei_ref, si_ref, q)
        prob = jnp.where(first, prob_ref[0:1, :], 0.0) + jnp.where(second, prob_ref[1:2, :], 0.0)
        weight = weight + jnp.sum(prob, axis=1, keepdims=True)
        masks.append(jnp.logical_or(first, second).astype(F32).astype(BF))
    rows = jnp.dot(jnp.concatenate(masks, axis=1), buf[...], preferred_element_type=F32)
    weight = jnp.where(t < 4, jnp.ones_like(weight), weight)
    out_ref[...] = (rows * weight).astype(BF)


def unpack(block, q, far):
    near = block[:, q * 8 : (q + 1) * 8, :].reshape(128, block.shape[2])
    rest = block[:, 16:24, :].reshape(128, block.shape[2])
    rest = jnp.dot(far, rest, preferred_element_type=F32).astype(BF)
    return jnp.concatenate([near, rest], axis=0)


def settle(low, high):
    near = low[0:128] + high[0:128]
    width = low.shape[1]
    far = low[128:256].reshape(16, 8, width)
    far = far + pltpu.roll(high[128:256].reshape(16, 8, width), 4, 1)
    pairs = far.reshape(8, 2, 8, width)
    row = lax.broadcasted_iota(jnp.int32, (8, 8, width), 1)
    rest = jnp.where(row < 4, pairs[:, 0], pltpu.roll(pairs[:, 1], 4, 1)).reshape(64, width)
    return jnp.concatenate([near, rest], axis=0)


def slot_term(delta, wg, wu):
    w = jnp.concatenate([wg.reshape(512, 256), wu.reshape(512, 256)], axis=1)
    return lax.dot_general(delta, w, LAST, preferred_element_type=F32)


def forward_kernel(core_ref, g_hbm, wg_hbm, wu_hbm, wd_hbm, out_ref, term_ref, buf, wg, wu, wd, sem):
    copies = [pltpu.make_async_copy(g_hbm.at[t], buf.at[t], sem.at[0, t]) for t in range(8)]
    down = [
        pltpu.make_async_copy(
            wd_hbm.at[:, pl.ds(q * 2048, 2048)], wd.at[:, pl.ds(q * 2048, 2048)], sem.at[1, q]
        )
        for q in range(2)
    ]
    first = [
        [
            pltpu.make_async_copy(
                src.at[pl.ds(q * 4, 4)], dst.at[pl.ds(q * 4, 4)], sem.at[2 + side, q]
            )
            for side, (src, dst) in enumerate(((wg_hbm, wg), (wu_hbm, wu)))
        ]
        for q in range(2)
    ]
    for copy in copies[4:8] + down + copies[0:4] + first[0] + first[1]:
        copy.start()

    def rows(units, q):
        return jnp.concatenate(
            [
                jnp.concatenate(
                    [
                        buf[t, :, q * 8 : (q + 1) * 8, :].reshape(128, 512),
                        buf[t, :, 16:24, :].reshape(128, 512),
                    ],
                    axis=0,
                )
                for t in units
            ],
            axis=1,
        )

    for copy in copies[4:8]:
        copy.wait()
    terms = []
    for q in range(2):
        down[q].wait()
        w = jnp.concatenate(
            [
                wd[:, (q * 4 + j) * 512 + unit * 128 : (q * 4 + j) * 512 + (unit + 1) * 128]
                for unit in range(4)
                for j in range(4)
            ],
            axis=1,
        )
        terms.append(
            lax.dot_general(rows(range(4, 8), q), w, LAST, preferred_element_type=F32)
        )
    back = settle(*terms)
    for copy in copies[0:4]:
        copy.wait()
    terms = []
    for q in range(2):
        for copy in first[q]:
            copy.wait()
        w = jnp.concatenate(
            [
                jnp.concatenate(
                    [m[q * 4 : (q + 1) * 4, unit].reshape(512, 256) for unit in range(4)], axis=0
                )
                for m in (wg, wu)
            ],
            axis=1,
        )
        terms.append(jnp.dot(rows(range(4), q), w, preferred_element_type=F32))
    both = settle(*terms)
    gate, up = both[:, 0:256], both[:, 256:512]
    sig = jax.nn.sigmoid(gate)
    act = gate * sig
    out_ref[:, 0:256] = (back * up * sig * (1.0 + gate * (1.0 - sig))).astype(BF)
    out_ref[:, 256:512] = (back * act).astype(BF)
    out_ref[:, 512:768] = (act * up).astype(BF)
    for i in range(4):
        k = 2 * i + 1 - core_ref[0]
        term_ref[i] = slot_term(out_ref[:, 0:512], wg[k], wu[k]).astype(BF)


def slot_kernel(core_ref, delta_ref, wg_hbm, wu_hbm, add_ref, out_ref, wg, wu, sem):
    copies = [
        [
            pltpu.make_async_copy(src.at[2 * i + core_ref[0]], dst.at[i], sem.at[side, i])
            for side, (src, dst) in enumerate(((wg_hbm, wg), (wu_hbm, wu)))
        ]
        for i in range(4)
    ]
    for group in copies:
        for copy in group:
            copy.start()
    for i in range(4):
        for copy in copies[i]:
            copy.wait()
        term = slot_term(delta_ref[:, 0:512], wg[i], wu[i])
        out_ref[i] = (term + add_ref[i].astype(F32)).astype(BF)


def pack_kernel(parts_ref, out_ref):
    total = parts_ref[0].astype(F32)
    for t in range(1, 4):
        total = total + parts_ref[t].astype(F32)
    rows = total.astype(BF)
    rest = jnp.zeros((128, 256), F32)
    for q in range(2):
        half = rows[:, q * 256 : (q + 1) * 256]
        out_ref[:, q * 8 : (q + 1) * 8, :] = half[0:128].reshape(16, 8, 256)
        rest += lax.dot_general(far_rows(q), half[128:192], FIRST, preferred_element_type=F32)
    out_ref[:, 16:24, :] = rest.astype(BF).reshape(16, 8, 256)


def combine_kernel(ei_ref, si_ref, ret_ref, out_ref):
    for q in range(2):
        first, second = picks(ei_ref, si_ref, q)
        mask = jnp.logical_or(first, second).astype(F32).astype(BF)
        out_ref[:, q * 256 : (q + 1) * 256] = lax.dot_general(
            mask, ret_ref[...], FIRST, preferred_element_type=F32
        ).astype(BF)


def corner_kernel(block_ref, out_ref):
    for q in range(2):
        x = unpack(block_ref[...], q, far_rows(q))
        for j in range(4):
            out_ref[q * 4 + j] = x[:, j * 128 : (j + 1) * 128]


def weight_kernel(t_ref, delta_ref, pair_hbm, side_hbm, side2_hbm, far_hbm, far2_hbm, gate_ref, up_ref, down_ref, buf, sem):
    t = t_ref[0]
    core = lax.rem(t, 2)
    chip = lax.div(t, 2)
    near = jnp.where(core == 0, 3, 1)
    places = [
        (pair_hbm.at[0], 0, core),
        (pair_hbm.at[1], 0, 1 - core),
        (side_hbm.at[0], near, core),
        (side_hbm.at[1], near, 1 - core),
        (side2_hbm.at[0], 4 - near, 1 - core),
        (side2_hbm.at[1], 4 - near, core),
        (far_hbm, 2, core),
        (far2_hbm, 2, 1 - core),
    ]
    copies = [
        pltpu.make_async_copy(src, buf.at[lax.rem(chip + shift, 4) * 2 + which], sem.at[i])
        for i, (src, shift, which) in enumerate(places)
    ]
    for copy in copies:
        copy.start()
    for copy in copies:
        copy.wait()
    tok = jnp.concatenate([buf[u].reshape(1536, 128) for u in range(4)], axis=1)
    both = lax.dot_general(tok, delta_ref[:, 0:512], FIRST, preferred_element_type=F32)
    gate_ref[...] = both[:, 0:256].astype(BF)
    up_ref[...] = both[:, 256:512].astype(BF)
    grad = jnp.concatenate([buf[4 + u].reshape(1536, 128) for u in range(4)], axis=1)
    down_ref[...] = lax.dot_general(
        delta_ref[:, 512:768], grad, FIRST, preferred_element_type=F32
    ).astype(BF)


def call(kernel, out, specs, scratch=(), flops=0, size=0, limit=67_043_328):
    single = not isinstance(out, (list, tuple))
    return pl.pallas_call(
        kernel,
        out_shape=out,
        in_specs=specs,
        out_specs=VM if single else [VM] * len(out),
        scratch_shapes=scratch,
        cost_estimate=pl.CostEstimate(flops=flops, bytes_accessed=size, transcendentals=0),
        compiler_params=pltpu.CompilerParams(vmem_limit_bytes=limit),
    )


def shape(dims, kind=BF):
    return jax.ShapeDtypeStruct(dims, kind)


def layer(tokens, out_grad, expert_index, slot_index, gate_probs, gate_weight, up_weight, down_weight):
    t = lax.axis_index("tensor").astype(jnp.int32).reshape(1)
    ei, si, prob = expert_index.T, slot_index.T, gate_probs.T
    wg = gate_weight.reshape(8, 4, 128, 256)
    wu = up_weight.reshape(8, 4, 128, 256)
    wd = down_weight[0]
    dma = pltpu.SemaphoreType.DMA

    sent = call(
        dispatch_kernel,
        shape((384, 512)),
        [SM, VM, VM, VM, HB, HB],
        [pltpu.VMEM((256, 512), BF), dma((8,))],
        flops=100_000_000,
        size=700_000,
    )(t, ei, si, prob, tokens, out_grad)
    block = lax.all_to_all(sent.reshape(16, 24, 512), "expert", 0, 0, tiled=True)
    whole = lax.all_gather(block.reshape(384, 512), "tensor", axis=0, tiled=True)

    corner = call(
        corner_kernel, shape((8, 192, 128)), [VM], flops=20_000_000, size=800_000
    )(block)
    mine = lax.all_to_all(corner, "dp", 0, 0, tiled=True)
    turned = lax.ppermute(mine, "tensor", SWAP)
    pair = jnp.concatenate([mine[None], turned[None]], axis=0)
    side = lax.ppermute(pair, "tensor", SIDE)
    far = lax.ppermute(mine, "tensor", FAR)
    whole, pair = lax.optimization_barrier((whole, pair))
    core = lax.bitwise_and(t, 1)
    delta, terms = call(
        forward_kernel,
        [shape((192, 768)), shape((4, 192, 512))],
        [SM, HB, HB, HB, HB],
        [
            pltpu.VMEM((8, 16, 24, 512), BF),
            pltpu.VMEM((8, 4, 128, 256), BF),
            pltpu.VMEM((8, 4, 128, 256), BF),
            pltpu.VMEM((256, 4096), BF),
            dma((4, 8)),
        ],
        flops=1_700_000_000,
        size=11_000_000,
    )(core, whole.reshape(8, 16, 24, 512), wg, wu, wd)
    side2 = lax.ppermute(side, "tensor", SWAP)
    far2 = lax.ppermute(far, "tensor", SWAP)
    deltas = lax.all_gather(delta, "dp", axis=0, tiled=True)

    terms = lax.ppermute(terms, "tensor", SWAP)
    terms = call(
        slot_kernel,
        shape((4, 192, 512)),
        [SM, VM, HB, HB, VM],
        [pltpu.VMEM((4, 4, 128, 256), BF), pltpu.VMEM((4, 4, 128, 256), BF), dma((2, 4))],
        flops=400_000_000,
        size=4_000_000,
    )(core, delta, wg, wu, terms)
    parts = lax.all_to_all(
        terms, "tensor", 0, 0, axis_index_groups=[[0, 2, 4, 6], [1, 3, 5, 7]], tiled=True
    )
    back = call(pack_kernel, shape((16, 24, 256)), [VM], flops=10_000_000, size=1_800_000)(parts)
    returned = lax.all_to_all(back, "expert", 0, 0, tiled=True)
    gate_grad, up_grad, down_grad = call(
        weight_kernel,
        [shape((512, 256)), shape((512, 256)), shape((256, 512))],
        [SM, VM, HB, HB, HB, HB, HB],
        [pltpu.VMEM((8, 8, 192, 128), BF), dma((8,))],
        flops=1_200_000_000,
        size=6_000_000,
    )(t, deltas, pair, side, side2, far, far2)
    returned, gate_grad = lax.optimization_barrier((returned, gate_grad))
    token_grad = call(
        combine_kernel, shape((128, 512)), [VM, VM, VM], flops=50_000_000, size=400_000
    )(ei, si, returned.reshape(384, 256))
    return (token_grad, gate_grad[None], up_grad[None], down_grad[None])


def solution(mesh):
    rows = P(("expert", "dp"), None)
    return jax.shard_map(
        layer,
        mesh=mesh,
        in_specs=(
            rows,
            rows,
            rows,
            rows,
            rows,
            P("expert", None, "tensor"),
            P("expert", None, "tensor"),
            P("expert", "tensor", None),
        ),
        out_specs=(
            P(("expert", "dp"), "tensor"),
            P("expert", "dp", "tensor"),
            P("expert", "dp", "tensor"),
            P("expert", "tensor", "dp"),
        ),
        check_vma=False,
    )
```

```python
import jax
import jax.numpy as jnp
from jax import lax
from jax.experimental import pallas as pl
from jax.experimental.pallas import tpu as pltpu
from jax.sharding import PartitionSpec as P


BF = jnp.bfloat16
F32 = jnp.float32
VM = pl.BlockSpec(memory_space=pltpu.VMEM)
HB = pl.BlockSpec(memory_space=pltpu.HBM)
SM = pl.BlockSpec(memory_space=pltpu.SMEM)
LAST = (((1,), (1,)), ((), ()))
FIRST = (((0,), (0,)), ((), ()))
TENSOR = 8
SIDE = [(t, (t + (2 if t % 2 == 0 else -2)) % TENSOR) for t in range(TENSOR)]
FAR = [(t, (t + 4) % TENSOR) for t in range(TENSOR)]
SWAP = [(t, t ^ 1) for t in range(TENSOR)]


def row_targets(ei, si, q):
    base = ei * 24
    near = base + q * 8 + si
    far = base + 16 + q * 4 + (si - 8)
    return jnp.where(si < 12, jnp.where(si < 8, near, far), -1)


def picks(ei_ref, si_ref, q):
    rows = lax.broadcasted_iota(jnp.int32, (384, 128), 0)
    target = row_targets(ei_ref[...], si_ref[...], q)
    return [rows == target[k : k + 1, :] for k in range(2)]


def far_rows(q):
    row = lax.broadcasted_iota(jnp.int32, (64, 128), 0)
    col = lax.broadcasted_iota(jnp.int32, (64, 128), 1)
    return (col == (row >> 2) * 8 + q * 4 + (row & 3)).astype(BF)


def dispatch_kernel(t_ref, ei_ref, si_ref, prob_ref, tok_hbm, grad_hbm, out_ref, buf, sem):
    t = t_ref[0]
    unit = lax.rem(t, 4)

    def fetch(src):
        for k in range(8):
            q, j = k // 4, k % 4
            pltpu.make_async_copy(
                src.at[:, pl.ds(pl.multiple_of(k * 512 + unit * 128, 128), 128)],
                buf.at[pl.ds(q * 128, 128), pl.ds(j * 128, 128)],
                sem.at[k],
            ).start()
        for k in range(8):
            q, j = k // 4, k % 4
            pltpu.make_async_copy(
                src.at[:, pl.ds(pl.multiple_of(k * 512 + unit * 128, 128), 128)],
                buf.at[pl.ds(q * 128, 128), pl.ds(j * 128, 128)],
                sem.at[k],
            ).wait()

    @pl.when(t < 4)
    def _():
        fetch(tok_hbm)

    @pl.when(t >= 4)
    def _():
        fetch(grad_hbm)

    masks, weight = [], jnp.zeros((384, 1), F32)
    for q in range(2):
        first, second = picks(ei_ref, si_ref, q)
        prob = jnp.where(first, prob_ref[0:1, :], 0.0) + jnp.where(second, prob_ref[1:2, :], 0.0)
        weight = weight + jnp.sum(prob, axis=1, keepdims=True)
        masks.append(jnp.logical_or(first, second).astype(F32).astype(BF))
    rows = jnp.dot(jnp.concatenate(masks, axis=1), buf[...], preferred_element_type=F32)
    weight = jnp.where(t < 4, jnp.ones_like(weight), weight)
    out_ref[...] = (rows * weight).astype(BF)


def unpack(block, q, far):
    near = block[:, q * 8 : (q + 1) * 8, :].reshape(128, block.shape[2])
    rest = block[:, 16:24, :].reshape(128, block.shape[2])
    rest = jnp.dot(far, rest, preferred_element_type=F32).astype(BF)
    return jnp.concatenate([near, rest], axis=0)


def settle(low, high):
    near = low[0:128] + high[0:128]
    width = low.shape[1]
    far = low[128:256].reshape(16, 8, width)
    far = far + pltpu.roll(high[128:256].reshape(16, 8, width), 4, 1)
    pairs = far.reshape(8, 2, 8, width)
    row = lax.broadcasted_iota(jnp.int32, (8, 8, width), 1)
    rest = jnp.where(row < 4, pairs[:, 0], pltpu.roll(pairs[:, 1], 4, 1)).reshape(64, width)
    return jnp.concatenate([near, rest], axis=0)


def forward_kernel(core_ref, g_hbm, wg_hbm, wu_hbm, wd_hbm, out_ref, term_ref, x, w, wd, sem):
    def load_rows(kind):
        copies = []
        for unit in range(4):
            t = kind * 4 + unit
            lanes = pl.ds(unit * 512, 512)
            for q in range(2):
                for part, row in enumerate((q * 8, 16)):
                    copies.append(
                        pltpu.make_async_copy(
                            g_hbm.at[t, :, pl.ds(row, 8), :],
                            x.at[kind, q, part, :, :, lanes],
                            sem.at[kind, unit * 4 + q * 2 + part],
                        )
                    )
        return copies

    def load_down(q):
        copies = []
        for j in range(4):
            for unit in range(4):
                copies.append(
                    pltpu.make_async_copy(
                        wd_hbm.at[:, pl.ds((q * 4 + j) * 512 + unit * 128, 128)],
                        wd.at[q, :, pl.ds(unit * 512 + j * 128, 128)],
                        sem.at[2 + q, unit * 4 + j],
                    )
                )
        return copies

    def load_first(q):
        copies = []
        for unit in range(4):
            for side, src in enumerate((wg_hbm, wu_hbm)):
                copies.append(
                    pltpu.make_async_copy(
                        src.at[pl.ds(q * 4, 4), unit],
                        w.at[q, unit, :, :, pl.ds(side * 256, 256)],
                        sem.at[4 + q, unit * 2 + side],
                    )
                )
        return copies

    grads, toks = load_rows(1), load_rows(0)
    down = [load_down(q) for q in range(2)]
    first = [load_first(q) for q in range(2)]
    for copy in grads + down[0] + down[1] + toks + first[0] + first[1]:
        copy.start()
    for copy in grads:
        copy.wait()
    terms = []
    for q in range(2):
        for copy in down[q]:
            copy.wait()
        terms.append(
            lax.dot_general(
                x[1, q].reshape(256, 2048), wd[q], LAST, preferred_element_type=F32
            )
        )
    back = settle(*terms)
    for copy in toks:
        copy.wait()
    terms = []
    for q in range(2):
        for copy in first[q]:
            copy.wait()
        terms.append(
            jnp.dot(
                x[0, q].reshape(256, 2048),
                w[q].reshape(2048, 512),
                preferred_element_type=F32,
            )
        )
    both = settle(*terms)
    gate, up = both[:, 0:256], both[:, 256:512]
    sig = jax.nn.sigmoid(gate)
    act = gate * sig
    deltas = jnp.concatenate(
        [
            (back * up * sig * (1.0 + gate * (1.0 - sig))).astype(BF),
            (back * act).astype(BF),
        ],
        axis=1,
    )
    out_ref[:, 0:512] = deltas
    out_ref[:, 512:768] = (act * up).astype(BF)
    for i in range(4):
        k = 2 * i + 1 - core_ref[0]
        block = w[i // 2, :, lax.rem(k, 4)].reshape(512, 512)
        term_ref[i] = lax.dot_general(
            deltas, block, LAST, preferred_element_type=F32
        ).astype(BF)


def slot_kernel(core_ref, delta_ref, wg_hbm, wu_hbm, out_ref, w, sem):
    copies = [
        [
            pltpu.make_async_copy(
                src.at[2 * i + core_ref[0]],
                w.at[i, :, :, pl.ds(side * 256, 256)],
                sem.at[side, i],
            )
            for side, src in enumerate((wg_hbm, wu_hbm))
        ]
        for i in range(4)
    ]
    for group in copies:
        for copy in group:
            copy.start()
    for i in range(4):
        for copy in copies[i]:
            copy.wait()
        out_ref[i] = lax.dot_general(
            delta_ref[:, 0:512], w[i].reshape(512, 512), LAST, preferred_element_type=F32
        ).astype(BF)


def pack_kernel(parts_ref, out_ref):
    total = parts_ref[0].astype(F32)
    for t in range(1, 4):
        total = total + parts_ref[t].astype(F32)
    rows = total.astype(BF)
    rest = jnp.zeros((128, 256), F32)
    for q in range(2):
        half = rows[:, q * 256 : (q + 1) * 256]
        out_ref[:, q * 8 : (q + 1) * 8, :] = half[0:128].reshape(16, 8, 256)
        rest += lax.dot_general(far_rows(q), half[128:192], FIRST, preferred_element_type=F32)
    out_ref[:, 16:24, :] = rest.astype(BF).reshape(16, 8, 256)


def combine_kernel(ei_ref, si_ref, ret_ref, out_ref):
    for q in range(2):
        first, second = picks(ei_ref, si_ref, q)
        mask = jnp.logical_or(first, second).astype(F32).astype(BF)
        out_ref[:, q * 256 : (q + 1) * 256] = lax.dot_general(
            mask, ret_ref[...], FIRST, preferred_element_type=F32
        ).astype(BF)


def corner_kernel(block_ref, out_ref):
    for q in range(2):
        x = unpack(block_ref[...], q, far_rows(q))
        for j in range(4):
            out_ref[q * 4 + j] = x[:, j * 128 : (j + 1) * 128]


def weight_kernel(t_ref, delta_ref, pair_hbm, side_hbm, side2_hbm, far_hbm, far2_hbm, gate_ref, up_ref, down_ref, buf, sem):
    t = t_ref[0]
    core = lax.rem(t, 2)
    chip = lax.div(t, 2)
    near = jnp.where(core == 0, 3, 1)
    places = [
        (pair_hbm.at[0], 0, core),
        (pair_hbm.at[1], 0, 1 - core),
        (side_hbm.at[0], near, core),
        (side_hbm.at[1], near, 1 - core),
        (side2_hbm.at[0], 4 - near, 1 - core),
        (side2_hbm.at[1], 4 - near, core),
        (far_hbm, 2, core),
        (far2_hbm, 2, 1 - core),
    ]
    copies = [
        pltpu.make_async_copy(src, buf.at[lax.rem(chip + shift, 4) * 2 + which], sem.at[i])
        for i, (src, shift, which) in enumerate(places)
    ]
    for copy in copies:
        copy.start()
    for copy in copies:
        copy.wait()
    tok = jnp.concatenate([buf[u].reshape(1536, 128) for u in range(4)], axis=1)
    both = lax.dot_general(tok, delta_ref[:, 0:512], FIRST, preferred_element_type=F32)
    gate_ref[...] = both[:, 0:256].astype(BF)
    up_ref[...] = both[:, 256:512].astype(BF)
    grad = jnp.concatenate([buf[4 + u].reshape(1536, 128) for u in range(4)], axis=1)
    down_ref[...] = lax.dot_general(
        delta_ref[:, 512:768], grad, FIRST, preferred_element_type=F32
    ).astype(BF)


def call(kernel, out, specs, scratch=(), flops=0, size=0, limit=67_043_328):
    single = not isinstance(out, (list, tuple))
    return pl.pallas_call(
        kernel,
        out_shape=out,
        in_specs=specs,
        out_specs=VM if single else [VM] * len(out),
        scratch_shapes=scratch,
        cost_estimate=pl.CostEstimate(flops=flops, bytes_accessed=size, transcendentals=0),
        compiler_params=pltpu.CompilerParams(vmem_limit_bytes=limit),
    )


def shape(dims, kind=BF):
    return jax.ShapeDtypeStruct(dims, kind)


def layer(tokens, out_grad, expert_index, slot_index, gate_probs, gate_weight, up_weight, down_weight):
    t = lax.axis_index("tensor").astype(jnp.int32).reshape(1)
    ei, si, prob = expert_index.T, slot_index.T, gate_probs.T
    wg = gate_weight.reshape(8, 4, 128, 256)
    wu = up_weight.reshape(8, 4, 128, 256)
    wd = down_weight[0]
    dma = pltpu.SemaphoreType.DMA

    sent = call(
        dispatch_kernel,
        shape((384, 512)),
        [SM, VM, VM, VM, HB, HB],
        [pltpu.VMEM((256, 512), BF), dma((8,))],
        flops=100_000_000,
        size=700_000,
    )(t, ei, si, prob, tokens, out_grad)
    block = lax.all_to_all(sent.reshape(16, 24, 512), "expert", 0, 0, tiled=True)
    whole = lax.all_gather(block.reshape(384, 512), "tensor", axis=0, tiled=True)

    corner = call(
        corner_kernel, shape((8, 192, 128)), [VM], flops=20_000_000, size=800_000
    )(block)
    mine = lax.all_to_all(corner, "dp", 0, 0, tiled=True)
    turned = lax.ppermute(mine, "tensor", SWAP)
    pair = jnp.concatenate([mine[None], turned[None]], axis=0)
    side = lax.ppermute(pair, "tensor", SIDE)
    far = lax.ppermute(mine, "tensor", FAR)
    whole, pair = lax.optimization_barrier((whole, pair))
    core = lax.bitwise_and(t, 1)
    delta, terms = call(
        forward_kernel,
        [shape((192, 768)), shape((4, 192, 512))],
        [SM, HB, HB, HB, HB],
        [
            pltpu.VMEM((2, 2, 2, 16, 8, 2048), BF),
            pltpu.VMEM((2, 4, 4, 128, 512), BF),
            pltpu.VMEM((2, 256, 2048), BF),
            dma((6, 16)),
        ],
        flops=1_700_000_000,
        size=11_000_000,
    )(core, whole.reshape(8, 16, 24, 512), wg, wu, wd)
    side2 = lax.ppermute(side, "tensor", SWAP)
    far2 = lax.ppermute(far, "tensor", SWAP)
    deltas = lax.all_gather(delta, "dp", axis=0, tiled=True)

    others = lax.ppermute(terms, "tensor", SWAP)
    terms = call(
        slot_kernel,
        shape((4, 192, 512)),
        [SM, VM, HB, HB],
        [pltpu.VMEM((4, 4, 128, 512), BF), dma((2, 4))],
        flops=400_000_000,
        size=4_000_000,
    )(core, delta, wg, wu)
    terms = (terms.astype(F32) + others.astype(F32)).astype(BF)
    parts = lax.all_to_all(
        terms, "tensor", 0, 0, axis_index_groups=[[0, 2, 4, 6], [1, 3, 5, 7]], tiled=True
    )
    back = call(pack_kernel, shape((16, 24, 256)), [VM], flops=10_000_000, size=1_800_000)(parts)
    returned = lax.all_to_all(back, "expert", 0, 0, tiled=True)
    gate_grad, up_grad, down_grad = call(
        weight_kernel,
        [shape((512, 256)), shape((512, 256)), shape((256, 512))],
        [SM, VM, HB, HB, HB, HB, HB],
        [pltpu.VMEM((8, 8, 192, 128), BF), dma((8,))],
        flops=1_200_000_000,
        size=6_000_000,
    )(t, deltas, pair, side, side2, far, far2)
    returned, gate_grad = lax.optimization_barrier((returned, gate_grad))
    token_grad = call(
        combine_kernel, shape((128, 512)), [VM, VM, VM], flops=50_000_000, size=400_000
    )(ei, si, returned.reshape(384, 256))
    return (token_grad, gate_grad[None], up_grad[None], down_grad[None])


def solution(mesh):
    rows = P(("expert", "dp"), None)
    return jax.shard_map(
        layer,
        mesh=mesh,
        in_specs=(
            rows,
            rows,
            rows,
            rows,
            rows,
            P("expert", None, "tensor"),
            P("expert", None, "tensor"),
            P("expert", "tensor", None),
        ),
        out_specs=(
            P(("expert", "dp"), "tensor"),
            P("expert", "dp", "tensor"),
            P("expert", "dp", "tensor"),
            P("expert", "tensor", "dp"),
        ),
        check_vma=False,
    )
```

```python
import jax
import jax.numpy as jnp
from jax import lax
from jax.experimental import pallas as pl
from jax.experimental.pallas import tpu as pltpu
from jax.sharding import PartitionSpec as P


BF = jnp.bfloat16
F32 = jnp.float32
VM = pl.BlockSpec(memory_space=pltpu.VMEM)
HB = pl.BlockSpec(memory_space=pltpu.HBM)
SM = pl.BlockSpec(memory_space=pltpu.SMEM)
LAST = (((1,), (1,)), ((), ()))
FIRST = (((0,), (0,)), ((), ()))
TENSOR = 8
SIDE = [(t, (t + (2 if t % 2 == 0 else -2)) % TENSOR) for t in range(TENSOR)]
FAR = [(t, (t + 4) % TENSOR) for t in range(TENSOR)]
SWAP = [(t, t ^ 1) for t in range(TENSOR)]


def row_targets(ei, si, q):
    base = ei * 24
    near = base + q * 8 + si
    far = base + 16 + q * 4 + (si - 8)
    return jnp.where(si < 12, jnp.where(si < 8, near, far), -1)


def picks(ei_ref, si_ref, q):
    rows = lax.broadcasted_iota(jnp.int32, (384, 128), 0)
    target = row_targets(ei_ref[...], si_ref[...], q)
    return [rows == target[k : k + 1, :] for k in range(2)]


def far_rows(q):
    row = lax.broadcasted_iota(jnp.int32, (64, 128), 0)
    col = lax.broadcasted_iota(jnp.int32, (64, 128), 1)
    return (col == (row >> 2) * 8 + q * 4 + (row & 3)).astype(BF)


def dispatch_kernel(t_ref, ei_ref, si_ref, prob_ref, tok_hbm, grad_hbm, out_ref, buf, sem):
    t = t_ref[0]
    unit = lax.rem(t, 4)

    def fetch(src):
        for k in range(8):
            q, j = k // 4, k % 4
            pltpu.make_async_copy(
                src.at[:, pl.ds(pl.multiple_of(k * 512 + unit * 128, 128), 128)],
                buf.at[pl.ds(q * 128, 128), pl.ds(j * 128, 128)],
                sem.at[k],
            ).start()
        for k in range(8):
            q, j = k // 4, k % 4
            pltpu.make_async_copy(
                src.at[:, pl.ds(pl.multiple_of(k * 512 + unit * 128, 128), 128)],
                buf.at[pl.ds(q * 128, 128), pl.ds(j * 128, 128)],
                sem.at[k],
            ).wait()

    @pl.when(t < 4)
    def _():
        fetch(tok_hbm)

    @pl.when(t >= 4)
    def _():
        fetch(grad_hbm)

    masks, weight = [], jnp.zeros((384, 1), F32)
    for q in range(2):
        first, second = picks(ei_ref, si_ref, q)
        prob = jnp.where(first, prob_ref[0:1, :], 0.0) + jnp.where(second, prob_ref[1:2, :], 0.0)
        weight = weight + jnp.sum(prob, axis=1, keepdims=True)
        masks.append(jnp.logical_or(first, second).astype(F32).astype(BF))
    rows = jnp.dot(jnp.concatenate(masks, axis=1), buf[...], preferred_element_type=F32)
    weight = jnp.where(t < 4, jnp.ones_like(weight), weight)
    out_ref[...] = (rows * weight).astype(BF)


def unpack(block, q, far):
    near = block[:, q * 8 : (q + 1) * 8, :].reshape(128, block.shape[2])
    rest = block[:, 16:24, :].reshape(128, block.shape[2])
    rest = jnp.dot(far, rest, preferred_element_type=F32).astype(BF)
    return jnp.concatenate([near, rest], axis=0)


def settle(low, high):
    near = low[0:128] + high[0:128]
    width = low.shape[1]
    far = low[128:256].reshape(16, 8, width)
    far = far + pltpu.roll(high[128:256].reshape(16, 8, width), 4, 1)
    pairs = far.reshape(8, 2, 8, width)
    row = lax.broadcasted_iota(jnp.int32, (8, 8, width), 1)
    rest = jnp.where(row < 4, pairs[:, 0], pltpu.roll(pairs[:, 1], 4, 1)).reshape(64, width)
    return jnp.concatenate([near, rest], axis=0)


def forward_kernel(g_hbm, wg_hbm, wu_hbm, wd_hbm, out_ref, buf, wg, wu, wd, sem):
    copies = [pltpu.make_async_copy(g_hbm.at[t], buf.at[t], sem.at[0, t]) for t in range(8)]
    down = [
        pltpu.make_async_copy(
            wd_hbm.at[:, pl.ds(q * 2048, 2048)], wd.at[:, pl.ds(q * 2048, 2048)], sem.at[1, q]
        )
        for q in range(2)
    ]
    first = [
        [
            pltpu.make_async_copy(
                src.at[pl.ds(q * 4, 4)], dst.at[pl.ds(q * 4, 4)], sem.at[2 + side, q]
            )
            for side, (src, dst) in enumerate(((wg_hbm, wg), (wu_hbm, wu)))
        ]
        for q in range(2)
    ]
    for copy in copies[4:8] + down + copies[0:4] + first[0] + first[1]:
        copy.start()

    def rows(units, q):
        return jnp.concatenate(
            [
                jnp.concatenate(
                    [
                        buf[t, :, q * 8 : (q + 1) * 8, :].reshape(128, 512),
                        buf[t, :, 16:24, :].reshape(128, 512),
                    ],
                    axis=0,
                )
                for t in units
            ],
            axis=1,
        )

    for copy in copies[4:8]:
        copy.wait()
    terms = []
    for q in range(2):
        down[q].wait()
        w = jnp.concatenate(
            [
                wd[:, (q * 4 + j) * 512 + unit * 128 : (q * 4 + j) * 512 + (unit + 1) * 128]
                for unit in range(4)
                for j in range(4)
            ],
            axis=1,
        )
        terms.append(
            lax.dot_general(rows(range(4, 8), q), w, LAST, preferred_element_type=F32)
        )
    back = settle(*terms)
    for copy in copies[0:4]:
        copy.wait()
    terms = []
    for q in range(2):
        for copy in first[q]:
            copy.wait()
        w = jnp.concatenate(
            [
                jnp.concatenate(
                    [m[q * 4 : (q + 1) * 4, unit].reshape(512, 256) for unit in range(4)], axis=0
                )
                for m in (wg, wu)
            ],
            axis=1,
        )
        terms.append(jnp.dot(rows(range(4), q), w, preferred_element_type=F32))
    both = settle(*terms)
    gate, up = both[:, 0:256], both[:, 256:512]
    sig = jax.nn.sigmoid(gate)
    act = gate * sig
    out_ref[:, 0:256] = (back * up * sig * (1.0 + gate * (1.0 - sig))).astype(BF)
    out_ref[:, 256:512] = (back * act).astype(BF)
    out_ref[:, 512:768] = (act * up).astype(BF)


def slot_kernel(core_ref, own_ref, other_ref, wg_hbm, wu_hbm, wg2_hbm, wu2_hbm, out_ref, w, sem):
    copies = [
        [
            pltpu.make_async_copy(
                src.at[2 * i + core_ref[0]], w.at[i, :, pl.ds(part * 256, 256)], sem.at[i, part]
            )
            for part, src in enumerate((wg_hbm, wu_hbm, wg2_hbm, wu2_hbm))
        ]
        for i in range(4)
    ]
    for group in copies:
        for copy in group:
            copy.start()
    deltas = jnp.concatenate([own_ref[:, 0:512], other_ref[:, 0:512]], axis=1)
    for i in range(4):
        for copy in copies[i]:
            copy.wait()
        out_ref[i] = lax.dot_general(deltas, w[i], LAST, preferred_element_type=F32).astype(BF)


def pack_kernel(parts_ref, out_ref):
    total = parts_ref[0].astype(F32)
    for t in range(1, 4):
        total = total + parts_ref[t].astype(F32)
    rows = total.astype(BF)
    rest = jnp.zeros((128, 256), F32)
    for q in range(2):
        half = rows[:, q * 256 : (q + 1) * 256]
        out_ref[:, q * 8 : (q + 1) * 8, :] = half[0:128].reshape(16, 8, 256)
        rest += lax.dot_general(far_rows(q), half[128:192], FIRST, preferred_element_type=F32)
    out_ref[:, 16:24, :] = rest.astype(BF).reshape(16, 8, 256)


def combine_kernel(ei_ref, si_ref, ret_ref, out_ref):
    for q in range(2):
        first, second = picks(ei_ref, si_ref, q)
        mask = jnp.logical_or(first, second).astype(F32).astype(BF)
        out_ref[:, q * 256 : (q + 1) * 256] = lax.dot_general(
            mask, ret_ref[...], FIRST, preferred_element_type=F32
        ).astype(BF)


def corner_kernel(block_ref, out_ref):
    for q in range(2):
        x = unpack(block_ref[...], q, far_rows(q))
        for j in range(4):
            out_ref[q * 4 + j] = x[:, j * 128 : (j + 1) * 128]


def weight_kernel(t_ref, delta_ref, pair_hbm, side_hbm, side2_hbm, far_hbm, far2_hbm, gate_ref, up_ref, down_ref, buf, sem):
    t = t_ref[0]
    core = lax.rem(t, 2)
    chip = lax.div(t, 2)
    near = jnp.where(core == 0, 3, 1)
    places = [
        (pair_hbm.at[0], 0, core),
        (pair_hbm.at[1], 0, 1 - core),
        (side_hbm.at[0], near, core),
        (side_hbm.at[1], near, 1 - core),
        (side2_hbm.at[0], 4 - near, 1 - core),
        (side2_hbm.at[1], 4 - near, core),
        (far_hbm, 2, core),
        (far2_hbm, 2, 1 - core),
    ]
    copies = [
        pltpu.make_async_copy(src, buf.at[lax.rem(chip + shift, 4) * 2 + which], sem.at[i])
        for i, (src, shift, which) in enumerate(places)
    ]
    for copy in copies:
        copy.start()
    for copy in copies:
        copy.wait()
    tok = jnp.concatenate([buf[u].reshape(1536, 128) for u in range(4)], axis=1)
    both = lax.dot_general(tok, delta_ref[:, 0:512], FIRST, preferred_element_type=F32)
    gate_ref[...] = both[:, 0:256].astype(BF)
    up_ref[...] = both[:, 256:512].astype(BF)
    grad = jnp.concatenate([buf[4 + u].reshape(1536, 128) for u in range(4)], axis=1)
    down_ref[...] = lax.dot_general(
        delta_ref[:, 512:768], grad, FIRST, preferred_element_type=F32
    ).astype(BF)


def call(kernel, out, specs, scratch=(), flops=0, size=0, limit=67_043_328):
    single = not isinstance(out, (list, tuple))
    return pl.pallas_call(
        kernel,
        out_shape=out,
        in_specs=specs,
        out_specs=VM if single else [VM] * len(out),
        scratch_shapes=scratch,
        cost_estimate=pl.CostEstimate(flops=flops, bytes_accessed=size, transcendentals=0),
        compiler_params=pltpu.CompilerParams(vmem_limit_bytes=limit),
    )


def shape(dims, kind=BF):
    return jax.ShapeDtypeStruct(dims, kind)


def layer(tokens, out_grad, expert_index, slot_index, gate_probs, gate_weight, up_weight, down_weight):
    t = lax.axis_index("tensor").astype(jnp.int32).reshape(1)
    ei, si, prob = expert_index.T, slot_index.T, gate_probs.T
    wg = gate_weight.reshape(8, 4, 128, 256)
    wu = up_weight.reshape(8, 4, 128, 256)
    wd = down_weight[0]
    dma = pltpu.SemaphoreType.DMA

    sent = call(
        dispatch_kernel,
        shape((384, 512)),
        [SM, VM, VM, VM, HB, HB],
        [pltpu.VMEM((256, 512), BF), dma((8,))],
        flops=100_000_000,
        size=700_000,
    )(t, ei, si, prob, tokens, out_grad)
    block = lax.all_to_all(sent.reshape(16, 24, 512), "expert", 0, 0, tiled=True)
    whole = lax.all_gather(block.reshape(384, 512), "tensor", axis=0, tiled=True)

    corner = call(
        corner_kernel, shape((8, 192, 128)), [VM], flops=20_000_000, size=800_000
    )(block)
    mine = lax.all_to_all(corner, "dp", 0, 0, tiled=True)
    turned = lax.ppermute(mine, "tensor", SWAP)
    pair = jnp.concatenate([mine[None], turned[None]], axis=0)
    side = lax.ppermute(pair, "tensor", SIDE)
    far = lax.ppermute(mine, "tensor", FAR)
    gate2 = lax.ppermute(gate_weight, "tensor", SWAP)
    up2 = lax.ppermute(up_weight, "tensor", SWAP)
    whole, pair = lax.optimization_barrier((whole, pair))
    core = lax.bitwise_and(t, 1)
    delta = call(
        forward_kernel,
        shape((192, 768)),
        [HB, HB, HB, HB],
        [
            pltpu.VMEM((8, 16, 24, 512), BF),
            pltpu.VMEM((8, 4, 128, 256), BF),
            pltpu.VMEM((8, 4, 128, 256), BF),
            pltpu.VMEM((256, 4096), BF),
            dma((4, 8)),
        ],
        flops=1_300_000_000,
        size=10_000_000,
    )(whole.reshape(8, 16, 24, 512), wg, wu, wd)
    side2 = lax.ppermute(side, "tensor", SWAP)
    far2 = lax.ppermute(far, "tensor", SWAP)
    deltas = lax.all_gather(delta, "dp", axis=0, tiled=True)

    delta2 = lax.ppermute(delta, "tensor", SWAP)
    blocks = (8, 512, 256)
    terms = call(
        slot_kernel,
        shape((4, 192, 512)),
        [SM, VM, VM, HB, HB, HB, HB],
        [pltpu.VMEM((4, 512, 1024), BF), dma((4, 4))],
        flops=800_000_000,
        size=6_000_000,
    )(core, delta, delta2, *(w.reshape(blocks) for w in (gate_weight, up_weight, gate2, up2)))
    parts = lax.all_to_all(
        terms, "tensor", 0, 0, axis_index_groups=[[0, 2, 4, 6], [1, 3, 5, 7]], tiled=True
    )
    back = call(pack_kernel, shape((16, 24, 256)), [VM], flops=10_000_000, size=1_800_000)(parts)
    returned = lax.all_to_all(back, "expert", 0, 0, tiled=True)
    gate_grad, up_grad, down_grad = call(
        weight_kernel,
        [shape((512, 256)), shape((512, 256)), shape((256, 512))],
        [SM, VM, HB, HB, HB, HB, HB],
        [pltpu.VMEM((8, 8, 192, 128), BF), dma((8,))],
        flops=1_200_000_000,
        size=6_000_000,
    )(t, deltas, pair, side, side2, far, far2)
    returned, gate_grad = lax.optimization_barrier((returned, gate_grad))
    token_grad = call(
        combine_kernel, shape((128, 512)), [VM, VM, VM], flops=50_000_000, size=400_000
    )(ei, si, returned.reshape(384, 256))
    return (token_grad, gate_grad[None], up_grad[None], down_grad[None])


def solution(mesh):
    rows = P(("expert", "dp"), None)
    return jax.shard_map(
        layer,
        mesh=mesh,
        in_specs=(
            rows,
            rows,
            rows,
            rows,
            rows,
            P("expert", None, "tensor"),
            P("expert", None, "tensor"),
            P("expert", "tensor", None),
        ),
        out_specs=(
            P(("expert", "dp"), "tensor"),
            P("expert", "dp", "tensor"),
            P("expert", "dp", "tensor"),
            P("expert", "tensor", "dp"),
        ),
        check_vma=False,
    )
```

```python
import jax
import jax.numpy as jnp
from jax import lax
from jax.experimental import pallas as pl
from jax.experimental.pallas import tpu as pltpu
from jax.sharding import PartitionSpec as P


BF = jnp.bfloat16
F32 = jnp.float32
VM = pl.BlockSpec(memory_space=pltpu.VMEM)
HB = pl.BlockSpec(memory_space=pltpu.HBM)
SM = pl.BlockSpec(memory_space=pltpu.SMEM)
LAST = (((1,), (1,)), ((), ()))
FIRST = (((0,), (0,)), ((), ()))
TENSOR = 8
SIDE = [(t, (t + (2 if t % 2 == 0 else -2)) % TENSOR) for t in range(TENSOR)]
FAR = [(t, (t + 4) % TENSOR) for t in range(TENSOR)]
SWAP = [(t, t ^ 1) for t in range(TENSOR)]


def row_targets(ei, si, q):
    base = ei * 24
    near = base + q * 8 + si
    far = base + 16 + q * 4 + (si - 8)
    return jnp.where(si < 12, jnp.where(si < 8, near, far), -1)


def picks(ei_ref, si_ref, q):
    rows = lax.broadcasted_iota(jnp.int32, (384, 128), 0)
    target = row_targets(ei_ref[...], si_ref[...], q)
    return [rows == target[k : k + 1, :] for k in range(2)]


def far_rows(q):
    row = lax.broadcasted_iota(jnp.int32, (64, 128), 0)
    col = lax.broadcasted_iota(jnp.int32, (64, 128), 1)
    return (col == (row >> 2) * 8 + q * 4 + (row & 3)).astype(BF)


def dispatch_kernel(t_ref, ei_ref, si_ref, prob_ref, tok_hbm, grad_hbm, out_ref, buf, sem):
    t = t_ref[0]
    unit = lax.rem(t, 4)

    def fetch(src):
        for k in range(8):
            q, j = k // 4, k % 4
            pltpu.make_async_copy(
                src.at[:, pl.ds(pl.multiple_of(k * 512 + unit * 128, 128), 128)],
                buf.at[pl.ds(q * 128, 128), pl.ds(j * 128, 128)],
                sem.at[k],
            ).start()
        for k in range(8):
            q, j = k // 4, k % 4
            pltpu.make_async_copy(
                src.at[:, pl.ds(pl.multiple_of(k * 512 + unit * 128, 128), 128)],
                buf.at[pl.ds(q * 128, 128), pl.ds(j * 128, 128)],
                sem.at[k],
            ).wait()

    @pl.when(t < 4)
    def _():
        fetch(tok_hbm)

    @pl.when(t >= 4)
    def _():
        fetch(grad_hbm)

    masks, weight = [], jnp.zeros((384, 1), F32)
    for q in range(2):
        first, second = picks(ei_ref, si_ref, q)
        prob = jnp.where(first, prob_ref[0:1, :], 0.0) + jnp.where(second, prob_ref[1:2, :], 0.0)
        weight = weight + jnp.sum(prob, axis=1, keepdims=True)
        masks.append(jnp.logical_or(first, second).astype(F32).astype(BF))
    rows = jnp.dot(jnp.concatenate(masks, axis=1), buf[...], preferred_element_type=F32)
    weight = jnp.where(t < 4, jnp.ones_like(weight), weight)
    out_ref[...] = (rows * weight).astype(BF)


def unpack(block, q, far):
    near = block[:, q * 8 : (q + 1) * 8, :].reshape(128, block.shape[2])
    rest = block[:, 16:24, :].reshape(128, block.shape[2])
    rest = jnp.dot(far, rest, preferred_element_type=F32).astype(BF)
    return jnp.concatenate([near, rest], axis=0)


def settle(low, high):
    near = low[0:128] + high[0:128]
    width = low.shape[1]
    far = low[128:256].reshape(16, 8, width)
    far = far + pltpu.roll(high[128:256].reshape(16, 8, width), 4, 1)
    pairs = far.reshape(8, 2, 8, width)
    row = lax.broadcasted_iota(jnp.int32, (8, 8, width), 1)
    rest = jnp.where(row < 4, pairs[:, 0], pltpu.roll(pairs[:, 1], 4, 1)).reshape(64, width)
    return jnp.concatenate([near, rest], axis=0)


def forward_kernel(g_hbm, wg_hbm, wu_hbm, wd_hbm, out_ref, buf, w, wd, sem):
    copies = [pltpu.make_async_copy(g_hbm.at[t], buf.at[t], sem.at[0, t]) for t in range(8)]
    down = [
        pltpu.make_async_copy(
            wd_hbm.at[:, pl.ds(q * 2048, 2048)], wd.at[:, pl.ds(q * 2048, 2048)], sem.at[1, q]
        )
        for q in range(2)
    ]
    first = [
        [
            pltpu.make_async_copy(
                src.at[pl.ds(q * 4, 4), unit],
                w.at[q, unit, :, :, pl.ds(side * 256, 256)],
                sem.at[2 + q, unit * 2 + side],
            )
            for unit in range(4)
            for side, src in enumerate((wg_hbm, wu_hbm))
        ]
        for q in range(2)
    ]
    for copy in copies[4:8] + down + copies[0:4] + first[0] + first[1]:
        copy.start()

    def rows(units, q):
        return jnp.concatenate(
            [
                jnp.concatenate(
                    [
                        buf[t, :, q * 8 : (q + 1) * 8, :].reshape(128, 512),
                        buf[t, :, 16:24, :].reshape(128, 512),
                    ],
                    axis=0,
                )
                for t in units
            ],
            axis=1,
        )

    for copy in copies[4:8]:
        copy.wait()
    terms = []
    for q in range(2):
        down[q].wait()
        wide = jnp.concatenate(
            [
                wd[:, (q * 4 + j) * 512 + unit * 128 : (q * 4 + j) * 512 + (unit + 1) * 128]
                for unit in range(4)
                for j in range(4)
            ],
            axis=1,
        )
        terms.append(
            lax.dot_general(rows(range(4, 8), q), wide, LAST, preferred_element_type=F32)
        )
    back = settle(*terms)
    for copy in copies[0:4]:
        copy.wait()
    terms = []
    for q in range(2):
        for copy in first[q]:
            copy.wait()
        terms.append(
            jnp.dot(
                rows(range(4), q), w[q].reshape(2048, 512), preferred_element_type=F32
            )
        )
    both = settle(*terms)
    gate, up = both[:, 0:256], both[:, 256:512]
    sig = jax.nn.sigmoid(gate)
    act = gate * sig
    out_ref[:, 0:256] = (back * up * sig * (1.0 + gate * (1.0 - sig))).astype(BF)
    out_ref[:, 256:512] = (back * act).astype(BF)
    out_ref[:, 512:768] = (act * up).astype(BF)


def slot_kernel(core_ref, own_ref, other_ref, wg_hbm, wu_hbm, wg2_hbm, wu2_hbm, out_ref, w, sem):
    copies = [
        [
            pltpu.make_async_copy(
                src.at[2 * i + core_ref[0]], w.at[i, :, pl.ds(part * 256, 256)], sem.at[i, part]
            )
            for part, src in enumerate((wg_hbm, wu_hbm, wg2_hbm, wu2_hbm))
        ]
        for i in range(4)
    ]
    for group in copies:
        for copy in group:
            copy.start()
    deltas = jnp.concatenate([own_ref[:, 0:512], other_ref[:, 0:512]], axis=1)
    for i in range(4):
        for copy in copies[i]:
            copy.wait()
        out_ref[i] = lax.dot_general(deltas, w[i], LAST, preferred_element_type=F32).astype(BF)


def pack_kernel(parts_ref, out_ref):
    total = parts_ref[0].astype(F32)
    for t in range(1, 4):
        total = total + parts_ref[t].astype(F32)
    rows = total.astype(BF)
    rest = jnp.zeros((128, 256), F32)
    for q in range(2):
        half = rows[:, q * 256 : (q + 1) * 256]
        out_ref[:, q * 8 : (q + 1) * 8, :] = half[0:128].reshape(16, 8, 256)
        rest += lax.dot_general(far_rows(q), half[128:192], FIRST, preferred_element_type=F32)
    out_ref[:, 16:24, :] = rest.astype(BF).reshape(16, 8, 256)


def combine_kernel(ei_ref, si_ref, ret_ref, out_ref):
    for q in range(2):
        first, second = picks(ei_ref, si_ref, q)
        mask = jnp.logical_or(first, second).astype(F32).astype(BF)
        out_ref[:, q * 256 : (q + 1) * 256] = lax.dot_general(
            mask, ret_ref[...], FIRST, preferred_element_type=F32
        ).astype(BF)


def corner_kernel(block_ref, out_ref):
    for q in range(2):
        x = unpack(block_ref[...], q, far_rows(q))
        for j in range(4):
            out_ref[q * 4 + j] = x[:, j * 128 : (j + 1) * 128]


def weight_kernel(t_ref, delta_ref, pair_hbm, side_hbm, side2_hbm, far_hbm, far2_hbm, gate_ref, up_ref, down_ref, buf, sem):
    t = t_ref[0]
    core = lax.rem(t, 2)
    chip = lax.div(t, 2)
    near = jnp.where(core == 0, 3, 1)
    places = [
        (pair_hbm.at[0], 0, core),
        (pair_hbm.at[1], 0, 1 - core),
        (side_hbm.at[0], near, core),
        (side_hbm.at[1], near, 1 - core),
        (side2_hbm.at[0], 4 - near, 1 - core),
        (side2_hbm.at[1], 4 - near, core),
        (far_hbm, 2, core),
        (far2_hbm, 2, 1 - core),
    ]
    copies = [
        pltpu.make_async_copy(src, buf.at[lax.rem(chip + shift, 4) * 2 + which], sem.at[i])
        for i, (src, shift, which) in enumerate(places)
    ]
    for copy in copies:
        copy.start()
    for copy in copies:
        copy.wait()
    tok = jnp.concatenate([buf[u].reshape(1536, 128) for u in range(4)], axis=1)
    both = lax.dot_general(tok, delta_ref[:, 0:512], FIRST, preferred_element_type=F32)
    gate_ref[...] = both[:, 0:256].astype(BF)
    up_ref[...] = both[:, 256:512].astype(BF)
    grad = jnp.concatenate([buf[4 + u].reshape(1536, 128) for u in range(4)], axis=1)
    down_ref[...] = lax.dot_general(
        delta_ref[:, 512:768], grad, FIRST, preferred_element_type=F32
    ).astype(BF)


ROOM = 67_043_328 - 16_000_000


def call(kernel, out, specs, scratch=(), flops=0, size=0, limit=67_043_328):
    single = not isinstance(out, (list, tuple))
    return pl.pallas_call(
        kernel,
        out_shape=out,
        in_specs=specs,
        out_specs=VM if single else [VM] * len(out),
        scratch_shapes=scratch,
        cost_estimate=pl.CostEstimate(flops=flops, bytes_accessed=size, transcendentals=0),
        compiler_params=pltpu.CompilerParams(vmem_limit_bytes=limit),
    )


def shape(dims, kind=BF):
    return jax.ShapeDtypeStruct(dims, kind)


def layer(tokens, out_grad, expert_index, slot_index, gate_probs, gate_weight, up_weight, down_weight):
    t = lax.axis_index("tensor").astype(jnp.int32).reshape(1)
    ei, si, prob = expert_index.T, slot_index.T, gate_probs.T
    wg = gate_weight.reshape(8, 4, 128, 256)
    wu = up_weight.reshape(8, 4, 128, 256)
    wd = down_weight[0]
    dma = pltpu.SemaphoreType.DMA

    sent = call(
        dispatch_kernel,
        shape((384, 512)),
        [SM, VM, VM, VM, HB, HB],
        [pltpu.VMEM((256, 512), BF), dma((8,))],
        flops=100_000_000,
        size=700_000,
    )(t, ei, si, prob, tokens, out_grad)
    block = lax.all_to_all(sent.reshape(16, 24, 512), "expert", 0, 0, tiled=True)
    whole = lax.all_gather(block.reshape(384, 512), "tensor", axis=0, tiled=True)

    corner = call(
        corner_kernel, shape((8, 192, 128)), [VM], flops=20_000_000, size=800_000
    )(block)
    mine = lax.all_to_all(corner, "dp", 0, 0, tiled=True)
    turned = lax.ppermute(mine, "tensor", SWAP)
    pair = jnp.concatenate([mine[None], turned[None]], axis=0)
    side = lax.ppermute(pair, "tensor", SIDE)
    far = lax.ppermute(mine, "tensor", FAR)
    gate2 = lax.ppermute(gate_weight, "tensor", SWAP)
    up2 = lax.ppermute(up_weight, "tensor", SWAP)
    whole, pair = lax.optimization_barrier((whole, pair))
    core = lax.bitwise_and(t, 1)
    delta = call(
        forward_kernel,
        shape((192, 768)),
        [HB, HB, HB, HB],
        [
            pltpu.VMEM((8, 16, 24, 512), BF),
            pltpu.VMEM((2, 4, 4, 128, 512), BF),
            pltpu.VMEM((256, 4096), BF),
            dma((4, 8)),
        ],
        flops=1_300_000_000,
        size=10_000_000,
    )(whole.reshape(8, 16, 24, 512), wg, wu, wd)
    deltas = lax.all_gather(delta, "dp", axis=0, tiled=True)

    delta2 = lax.ppermute(delta, "tensor", SWAP)
    blocks = (8, 512, 256)
    terms = call(
        slot_kernel,
        shape((4, 192, 512)),
        [SM, VM, VM, HB, HB, HB, HB],
        [pltpu.VMEM((4, 512, 1024), BF), dma((4, 4))],
        flops=800_000_000,
        size=6_000_000,
        limit=ROOM,
    )(core, delta, delta2, *(w.reshape(blocks) for w in (gate_weight, up_weight, gate2, up2)))
    parts = lax.all_to_all(
        terms, "tensor", 0, 0, axis_index_groups=[[0, 2, 4, 6], [1, 3, 5, 7]], tiled=True
    )
    back = call(pack_kernel, shape((16, 24, 256)), [VM], flops=10_000_000, size=1_800_000, limit=32 << 20)(parts)
    side, far, back = lax.optimization_barrier((side, far, back))
    side2 = lax.ppermute(side, "tensor", SWAP)
    far2 = lax.ppermute(far, "tensor", SWAP)
    returned = lax.all_to_all(back, "expert", 0, 0, tiled=True)
    gate_grad, up_grad, down_grad = call(
        weight_kernel,
        [shape((512, 256)), shape((512, 256)), shape((256, 512))],
        [SM, VM, HB, HB, HB, HB, HB],
        [pltpu.VMEM((8, 8, 192, 128), BF), dma((8,))],
        flops=1_200_000_000,
        size=6_000_000,
    )(t, deltas, pair, side, side2, far, far2)
    returned, gate_grad = lax.optimization_barrier((returned, gate_grad))
    token_grad = call(
        combine_kernel, shape((128, 512)), [VM, VM, VM], flops=50_000_000, size=400_000
    )(ei, si, returned.reshape(384, 256))
    return (token_grad, gate_grad[None], up_grad[None], down_grad[None])


def solution(mesh):
    rows = P(("expert", "dp"), None)
    return jax.shard_map(
        layer,
        mesh=mesh,
        in_specs=(
            rows,
            rows,
            rows,
            rows,
            rows,
            P("expert", None, "tensor"),
            P("expert", None, "tensor"),
            P("expert", "tensor", None),
        ),
        out_specs=(
            P(("expert", "dp"), "tensor"),
            P("expert", "dp", "tensor"),
            P("expert", "dp", "tensor"),
            P("expert", "tensor", "dp"),
        ),
        check_vma=False,
    )
```

```python
import jax
import jax.numpy as jnp
from jax import lax
from jax.experimental import pallas as pl
from jax.experimental.pallas import tpu as pltpu
from jax.sharding import PartitionSpec as P


BF = jnp.bfloat16
F32 = jnp.float32
VM = pl.BlockSpec(memory_space=pltpu.VMEM)
HB = pl.BlockSpec(memory_space=pltpu.HBM)
SM = pl.BlockSpec(memory_space=pltpu.SMEM)
LAST = (((1,), (1,)), ((), ()))
FIRST = (((0,), (0,)), ((), ()))
TENSOR = 8
SIDE = [(t, (t + (2 if t % 2 == 0 else -2)) % TENSOR) for t in range(TENSOR)]
FAR = [(t, (t + 4) % TENSOR) for t in range(TENSOR)]
SWAP = [(t, t ^ 1) for t in range(TENSOR)]


def row_targets(ei, si, q):
    base = ei * 24
    near = base + q * 8 + si
    far = base + 16 + q * 4 + (si - 8)
    return jnp.where(si < 12, jnp.where(si < 8, near, far), -1)


def picks(ei_ref, si_ref, q):
    rows = lax.broadcasted_iota(jnp.int32, (384, 128), 0)
    target = row_targets(ei_ref[...], si_ref[...], q)
    return [rows == target[k : k + 1, :] for k in range(2)]


def far_rows(q):
    row = lax.broadcasted_iota(jnp.int32, (64, 128), 0)
    col = lax.broadcasted_iota(jnp.int32, (64, 128), 1)
    return (col == (row >> 2) * 8 + q * 4 + (row & 3)).astype(BF)


def dispatch_kernel(t_ref, ei_ref, si_ref, prob_ref, tok_hbm, grad_hbm, out_ref, buf, sem):
    t = t_ref[0]
    unit = lax.rem(t, 4)

    def fetch(src):
        for k in range(8):
            q, j = k // 4, k % 4
            pltpu.make_async_copy(
                src.at[:, pl.ds(pl.multiple_of(k * 512 + unit * 128, 128), 128)],
                buf.at[pl.ds(q * 128, 128), pl.ds(j * 128, 128)],
                sem.at[k],
            ).start()
        for k in range(8):
            q, j = k // 4, k % 4
            pltpu.make_async_copy(
                src.at[:, pl.ds(pl.multiple_of(k * 512 + unit * 128, 128), 128)],
                buf.at[pl.ds(q * 128, 128), pl.ds(j * 128, 128)],
                sem.at[k],
            ).wait()

    @pl.when(t < 4)
    def _():
        fetch(tok_hbm)

    @pl.when(t >= 4)
    def _():
        fetch(grad_hbm)

    masks, weight = [], jnp.zeros((384, 1), F32)
    for q in range(2):
        first, second = picks(ei_ref, si_ref, q)
        prob = jnp.where(first, prob_ref[0:1, :], 0.0) + jnp.where(second, prob_ref[1:2, :], 0.0)
        weight = weight + jnp.sum(prob, axis=1, keepdims=True)
        masks.append(jnp.logical_or(first, second).astype(F32).astype(BF))
    rows = jnp.dot(jnp.concatenate(masks, axis=1), buf[...], preferred_element_type=F32)
    weight = jnp.where(t < 4, jnp.ones_like(weight), weight)
    out_ref[...] = (rows * weight).astype(BF)


def unpack(block, q, far):
    near = block[:, q * 8 : (q + 1) * 8, :].reshape(128, block.shape[2])
    rest = block[:, 16:24, :].reshape(128, block.shape[2])
    rest = jnp.dot(far, rest, preferred_element_type=F32).astype(BF)
    return jnp.concatenate([near, rest], axis=0)


def settle(low, high):
    near = low[0:128] + high[0:128]
    width = low.shape[1]
    far = low[128:256].reshape(16, 8, width)
    far = far + pltpu.roll(high[128:256].reshape(16, 8, width), 4, 1)
    pairs = far.reshape(8, 2, 8, width)
    row = lax.broadcasted_iota(jnp.int32, (8, 8, width), 1)
    rest = jnp.where(row < 4, pairs[:, 0], pltpu.roll(pairs[:, 1], 4, 1)).reshape(64, width)
    return jnp.concatenate([near, rest], axis=0)


def forward_kernel(g_hbm, wg_hbm, wu_hbm, wd_hbm, out_ref, buf, w, wd, sem):
    copies = [pltpu.make_async_copy(g_hbm.at[t], buf.at[t], sem.at[0, t]) for t in range(8)]
    down = [
        pltpu.make_async_copy(
            wd_hbm.at[:, pl.ds(q * 2048, 2048)], wd.at[:, pl.ds(q * 2048, 2048)], sem.at[1, q]
        )
        for q in range(2)
    ]
    first = [
        [
            pltpu.make_async_copy(
                src.at[pl.ds(q * 4, 4), unit],
                w.at[q, unit, :, :, pl.ds(side * 256, 256)],
                sem.at[2 + q, unit * 2 + side],
            )
            for unit in range(4)
            for side, src in enumerate((wg_hbm, wu_hbm))
        ]
        for q in range(2)
    ]
    for copy in copies[4:8] + down + copies[0:4] + first[0] + first[1]:
        copy.start()

    def rows(units, q):
        return jnp.concatenate(
            [
                jnp.concatenate(
                    [
                        buf[t, :, q * 8 : (q + 1) * 8, :].reshape(128, 512),
                        buf[t, :, 16:24, :].reshape(128, 512),
                    ],
                    axis=0,
                )
                for t in units
            ],
            axis=1,
        )

    for copy in copies[4:8]:
        copy.wait()
    terms = []
    for q in range(2):
        down[q].wait()
        wide = jnp.concatenate(
            [
                wd[:, (q * 4 + j) * 512 + unit * 128 : (q * 4 + j) * 512 + (unit + 1) * 128]
                for unit in range(4)
                for j in range(4)
            ],
            axis=1,
        )
        terms.append(
            lax.dot_general(rows(range(4, 8), q), wide, LAST, preferred_element_type=F32)
        )
    back = settle(*terms)
    for copy in copies[0:4]:
        copy.wait()
    terms = []
    for q in range(2):
        for copy in first[q]:
            copy.wait()
        terms.append(
            jnp.dot(
                rows(range(4), q), w[q].reshape(2048, 512), preferred_element_type=F32
            )
        )
    both = settle(*terms)
    gate, up = both[:, 0:256], both[:, 256:512]
    sig = jax.nn.sigmoid(gate)
    act = gate * sig
    out_ref[:, 0:256] = (back * up * sig * (1.0 + gate * (1.0 - sig))).astype(BF)
    out_ref[:, 256:512] = (back * act).astype(BF)
    out_ref[:, 512:768] = (act * up).astype(BF)


def slot_kernel(core_ref, own_ref, other_ref, wg_hbm, wu_hbm, wg2_hbm, wu2_hbm, out_ref, w, sem):
    copies = [
        [
            pltpu.make_async_copy(
                src.at[2 * i + core_ref[0]], w.at[i, :, pl.ds(part * 256, 256)], sem.at[i, part]
            )
            for part, src in enumerate((wg_hbm, wu_hbm, wg2_hbm, wu2_hbm))
        ]
        for i in range(4)
    ]
    for group in copies:
        for copy in group:
            copy.start()
    deltas = jnp.concatenate([own_ref[:, 0:512], other_ref[:, 0:512]], axis=1)
    for i in range(4):
        for copy in copies[i]:
            copy.wait()
        out_ref[i] = lax.dot_general(deltas, w[i], LAST, preferred_element_type=F32).astype(BF)


def pack_kernel(parts_ref, out_ref):
    total = parts_ref[0].astype(F32)
    for t in range(1, 4):
        total = total + parts_ref[t].astype(F32)
    rows = total.astype(BF)
    rest = jnp.zeros((128, 256), F32)
    for q in range(2):
        half = rows[:, q * 256 : (q + 1) * 256]
        out_ref[:, q * 8 : (q + 1) * 8, :] = half[0:128].reshape(16, 8, 256)
        rest += lax.dot_general(far_rows(q), half[128:192], FIRST, preferred_element_type=F32)
    out_ref[:, 16:24, :] = rest.astype(BF).reshape(16, 8, 256)


def combine_kernel(ei_ref, si_ref, ret_ref, out_ref):
    for q in range(2):
        first, second = picks(ei_ref, si_ref, q)
        mask = jnp.logical_or(first, second).astype(F32).astype(BF)
        out_ref[:, q * 256 : (q + 1) * 256] = lax.dot_general(
            mask, ret_ref[...], FIRST, preferred_element_type=F32
        ).astype(BF)


def corner_kernel(block_ref, out_ref):
    for q in range(2):
        x = unpack(block_ref[...], q, far_rows(q))
        for j in range(4):
            out_ref[q * 4 + j] = x[:, j * 128 : (j + 1) * 128]


def weight_kernel(t_ref, delta_hbm, pair_hbm, side_hbm, side2_hbm, far_hbm, far2_hbm, gate_ref, up_ref, down_ref, buf, delta_ref, sem):
    t = t_ref[0]
    core = lax.rem(t, 2)
    chip = lax.div(t, 2)
    near = jnp.where(core == 0, 3, 1)
    places = [
        (pair_hbm.at[0], 0, core),
        (pair_hbm.at[1], 0, 1 - core),
        (side_hbm.at[0], near, core),
        (side_hbm.at[1], near, 1 - core),
        (side2_hbm.at[0], 4 - near, 1 - core),
        (side2_hbm.at[1], 4 - near, core),
        (far_hbm, 2, core),
        (far2_hbm, 2, 1 - core),
    ]
    copies = [
        pltpu.make_async_copy(src, buf.at[lax.rem(chip + shift, 4) * 2 + which], sem.at[i])
        for i, (src, shift, which) in enumerate(places)
    ]
    copies.append(pltpu.make_async_copy(delta_hbm, delta_ref, sem.at[8]))
    for copy in copies:
        copy.start()
    for copy in copies:
        copy.wait()
    tok = jnp.concatenate([buf[u].reshape(1536, 128) for u in range(4)], axis=1)
    both = lax.dot_general(tok, delta_ref[:, 0:512], FIRST, preferred_element_type=F32)
    gate_ref[...] = both[:, 0:256].astype(BF)
    up_ref[...] = both[:, 256:512].astype(BF)
    grad = jnp.concatenate([buf[4 + u].reshape(1536, 128) for u in range(4)], axis=1)
    down_ref[...] = lax.dot_general(
        delta_ref[:, 512:768], grad, FIRST, preferred_element_type=F32
    ).astype(BF)


ROOM = 67_043_328 - 16_000_000


def call(kernel, out, specs, scratch=(), flops=0, size=0, limit=67_043_328):
    single = not isinstance(out, (list, tuple))
    return pl.pallas_call(
        kernel,
        out_shape=out,
        in_specs=specs,
        out_specs=VM if single else [VM] * len(out),
        scratch_shapes=scratch,
        cost_estimate=pl.CostEstimate(flops=flops, bytes_accessed=size, transcendentals=0),
        compiler_params=pltpu.CompilerParams(vmem_limit_bytes=limit),
    )


def shape(dims, kind=BF):
    return jax.ShapeDtypeStruct(dims, kind)


def layer(tokens, out_grad, expert_index, slot_index, gate_probs, gate_weight, up_weight, down_weight):
    t = lax.axis_index("tensor").astype(jnp.int32).reshape(1)
    ei, si, prob = expert_index.T, slot_index.T, gate_probs.T
    wg = gate_weight.reshape(8, 4, 128, 256)
    wu = up_weight.reshape(8, 4, 128, 256)
    wd = down_weight[0]
    dma = pltpu.SemaphoreType.DMA

    sent = call(
        dispatch_kernel,
        shape((384, 512)),
        [SM, VM, VM, VM, HB, HB],
        [pltpu.VMEM((256, 512), BF), dma((8,))],
        flops=100_000_000,
        size=700_000,
    )(t, ei, si, prob, tokens, out_grad)
    block = lax.all_to_all(sent.reshape(16, 24, 512), "expert", 0, 0, tiled=True)
    whole = lax.all_gather(block.reshape(384, 512), "tensor", axis=0, tiled=True)

    corner = call(
        corner_kernel, shape((8, 192, 128)), [VM], flops=20_000_000, size=800_000
    )(block)
    mine = lax.all_to_all(corner, "dp", 0, 0, tiled=True)
    turned = lax.ppermute(mine, "tensor", SWAP)
    pair = jnp.concatenate([mine[None], turned[None]], axis=0)
    side = lax.ppermute(pair, "tensor", SIDE)
    far = lax.ppermute(mine, "tensor", FAR)
    gate2 = lax.ppermute(gate_weight, "tensor", SWAP)
    up2 = lax.ppermute(up_weight, "tensor", SWAP)
    whole, pair = lax.optimization_barrier((whole, pair))
    core = lax.bitwise_and(t, 1)
    delta = call(
        forward_kernel,
        shape((192, 768)),
        [HB, HB, HB, HB],
        [
            pltpu.VMEM((8, 16, 24, 512), BF),
            pltpu.VMEM((2, 4, 4, 128, 512), BF),
            pltpu.VMEM((256, 4096), BF),
            dma((4, 8)),
        ],
        flops=1_300_000_000,
        size=10_000_000,
    )(whole.reshape(8, 16, 24, 512), wg, wu, wd)
    deltas = lax.all_gather(delta, "dp", axis=0, tiled=True)

    delta2 = lax.ppermute(delta, "tensor", SWAP)
    blocks = (8, 512, 256)
    terms = call(
        slot_kernel,
        shape((4, 192, 512)),
        [SM, VM, VM, HB, HB, HB, HB],
        [pltpu.VMEM((4, 512, 1024), BF), dma((4, 4))],
        flops=800_000_000,
        size=6_000_000,
        limit=ROOM,
    )(core, delta, delta2, *(w.reshape(blocks) for w in (gate_weight, up_weight, gate2, up2)))
    parts = lax.all_to_all(
        terms, "tensor", 0, 0, axis_index_groups=[[0, 2, 4, 6], [1, 3, 5, 7]], tiled=True
    )
    back = call(pack_kernel, shape((16, 24, 256)), [VM], flops=10_000_000, size=1_800_000, limit=32 << 20)(parts)
    side, far, back = lax.optimization_barrier((side, far, back))
    side2 = lax.ppermute(side, "tensor", SWAP)
    far2 = lax.ppermute(far, "tensor", SWAP)
    returned = lax.all_to_all(back, "expert", 0, 0, tiled=True)
    gate_grad, up_grad, down_grad = call(
        weight_kernel,
        [shape((512, 256)), shape((512, 256)), shape((256, 512))],
        [SM, HB, HB, HB, HB, HB, HB],
        [pltpu.VMEM((8, 8, 192, 128), BF), pltpu.VMEM((1536, 768), BF), dma((9,))],
        flops=1_200_000_000,
        size=6_000_000,
    )(t, deltas, pair, side, side2, far, far2)
    returned, gate_grad = lax.optimization_barrier((returned, gate_grad))
    token_grad = call(
        combine_kernel, shape((128, 512)), [VM, VM, VM], flops=50_000_000, size=400_000
    )(ei, si, returned.reshape(384, 256))
    return (token_grad, gate_grad[None], up_grad[None], down_grad[None])


def solution(mesh):
    rows = P(("expert", "dp"), None)
    return jax.shard_map(
        layer,
        mesh=mesh,
        in_specs=(
            rows,
            rows,
            rows,
            rows,
            rows,
            P("expert", None, "tensor"),
            P("expert", None, "tensor"),
            P("expert", "tensor", None),
        ),
        out_specs=(
            P(("expert", "dp"), "tensor"),
            P("expert", "dp", "tensor"),
            P("expert", "dp", "tensor"),
            P("expert", "tensor", "dp"),
        ),
        check_vma=False,
    )
```
